256 devices in a mesh: slab: 64 (over x, z, core), geo: 4 (over y).
Axes of the slice: x: 4, y: 4, z: 8, core: 2. Of those that a mesh axis runs over, the one named last changes fastest.
Arguments:
- enc_feat: float32 [32768, 32, 128], P(('geo', 'slab')), parts along dimension 0, may hold values from -6 to 6
- enc_pos: float32 [32768, 3, 128], P(('geo', 'slab')), parts along dimension 0, may hold values from -1 to 1
- enc_dest: int32 [32768, 1], P(('geo', 'slab')), parts along dimension 0, may hold values from 0 to 63; in each aligned block of 128 rows (0 to 127, 128 to 255, ...) at most 6 rows name the same one
- enc_line: int32 [32768], P(('geo', 'slab')), parts along dimension 0, may hold values from 0 to 255
- dec_pos: float32 [32768, 3, 128], P(('geo', 'slab')), parts along dimension 0, may hold values from -1 to 1
- dec_dest: int32 [32768, 1], P(('geo', 'slab')), parts along dimension 0, may hold values from 0 to 63; in each aligned block of 128 rows (0 to 127, 128 to 255, ...) at most 6 rows name the same one
- dec_line: int32 [32768], P(('geo', 'slab')), parts along dimension 0, may hold values from 0 to 255
- mode_weight: bfloat16 [64, 64, 33, 2048], P(None, 'slab'), may hold values from -3 to 3
- skip_weight: float32 [32, 32], replicated, may hold values from -1 to 1
- skip_bias: float32 [32], replicated, may hold values from -3 to 3
- dec_weight: float32 [32, 32], replicated, may hold values from -1 to 1
- out_weight: float32 [32], replicated, may hold values from -1 to 1
Outputs:
- pressure: float32 [32768, 128], P(('geo', 'slab')), parts along dimension 0
The draws below stay inside these ranges and needn't reach their ends.
There are 4 independent parts, one for each index of `geo`. The reference program is written for one: setup_inputs(seed, part) draws one part's arguments, and reference() takes and returns one part's arrays. A program takes and returns all parts, laid end to end along the dimension named above; an argument that names none is the same for every part. Nothing has to cross between parts.
Inputs may be any that keep to these rules, and one draw needn't show every extreme that they name: `enc_dest`: among the blocks of one device each slab number appears at most 6 times; some device names some slab exactly 6 times. `dec_dest`: among the blocks of one device each slab number appears at most 6 times; some device names some slab exactly 6 times.
All inputs are finite; a program needn't handle non-finite values.
Results may differ from the reference program's by a relative error of at most 0.0003.
Values sent between devices are 32-bit elements; how exact they have to be, the bound alone decides.
A program may use at most 128 MiB of HBM per device.

```python
import math
import jax
import jax.numpy as jnp
import numpy as np
from jax import lax

C = 32
NX = 128
NY = 128
NZ = 128
MX = 64
MY = 64
MZ = 33
PB = 128
BLK_DEV = 128
OWNERS = 64
BLOCKS = 8192
CAP = 6
LINES_DEV = 256
N_SLAB = 64


def place_ends(array, key, least, high):
    place = [jax.random.randint(jax.random.fold_in(key, axis), (), 0, length) for axis, length in enumerate(array.shape)]
    main_axis = array.shape.index(max(array.shape))
    neighbour = place[:main_axis] + [(place[main_axis] + 1) % array.shape[main_axis]] + place[main_axis + 1:]
    return array.at[tuple(place)].set(least).at[tuple(neighbour)].set(high)


def steps_of(key, dims, pieces, low, largest):
    gain, own = 1.0, jax.random.fold_in(key, 6)
    for position, shards_of in pieces:
        steps = jnp.exp(jax.random.uniform(jax.random.fold_in(own, position), (shards_of,), jnp.float32, low / len(pieces), largest / len(pieces)))
        gain = gain * jnp.repeat(steps, dims[position] // shards_of).reshape([-1 if axis == position else 1 for axis in range(len(dims))])
    return gain


def routed_block(own_key, own, number, rows, count, top, most, lean):
    ranking = jax.random.permutation(own_key, count)
    crowded, usual = load_shares(count, rows * top, most, lean, True), load_shares(count, rows * top, most, lean, False)
    places = jnp.arange(count)

    def named(sizes, rotation):
        used = int((sizes > 0).sum())
        fixed = max(1, used // 4)
        passed = fixed + (places - fixed + rotation * (used - fixed)) % max(1, count - fixed)
        return jnp.zeros((count,), jnp.int32).at[ranking[jnp.where(places < fixed, places, passed)]].set(jnp.asarray(sizes, jnp.int32))

    sizes = jnp.where(number % 4 == 0, named(crowded, number // 4), named(usual, number - number // 4 - 1))
    mixed = jax.random.permutation(jax.random.fold_in(own, 3), count)
    giver, receiver = mixed[0:count // 2 * 2:2], mixed[1:count // 2 * 2:2]
    room = jnp.minimum(sizes[giver] - 1, most - sizes[receiver]) // 2
    room = jnp.where((giver == ranking[0]) | (receiver == ranking[0]) | (sizes[receiver] == 0), 0, jnp.maximum(room, 0))
    passed = jax.random.randint(jax.random.fold_in(own, 4), (count // 2,), 0, 1 << 20) % (room + 1)
    sizes = sizes.at[giver].add(-passed).at[receiver].add(passed)
    members = jnp.searchsorted(jnp.cumsum(sizes), jnp.arange(rows * top), side="right").astype(jnp.int32)
    grid = members.reshape(top, rows).T
    grid = grid[jax.random.permutation(jax.random.fold_in(own, 1), rows)]
    rotation = jax.random.randint(jax.random.fold_in(own, 2), (rows, 1), 0, top)
    return jnp.take_along_axis(grid, (jnp.arange(top)[None, :] + rotation) % top, axis=1)


def load_shares(number_of, total, reach, lean, full):
    portions = [(1 << 20) // math.isqrt(rank ** lean) + 1 for rank in range(1, number_of + 1)]
    largest = reach if full else min(reach, max(-(-total // number_of), total * portions[0] // sum(portions)))
    least = 1 if total - largest >= number_of - 1 else 0
    given, spare = [largest] + [least] * (number_of - 1), total - largest - least * (number_of - 1)
    while spare > 0:
        candidates = [i for i in range(1, number_of) if given[i] < largest] or [i for i in range(1, number_of) if given[i] < reach]
        pool, remaining = sum([portions[i] for i in candidates]), spare
        for i in candidates:
            more = min(reach - given[i], max(1, remaining * portions[i] // pool), spare)
            given[i] = given[i] + more
            spare = spare - more
    return np.array(given)


def normal_values(key, extent, scale, limit, pieces=(), held_as=jnp.bfloat16):
    gain = steps_of(key, extent, pieces, -0.22, 0.18) if pieces else 1.0
    array = jax.random.normal(key, extent, jnp.float32) * scale * gain
    return jnp.minimum(jnp.maximum(array, -limit), limit).astype(held_as)


def setup_inputs(seed: int = 0, part: int = 0) -> dict:
    key_of = jax.random.split(jax.random.key(seed), 13)
    part_keys = jax.random.split(jax.random.fold_in(key_of[12], part), 13)
    enc_feat = normal_values(part_keys[0], (BLOCKS, C, PB), 1.0, 6.0, ((0, 64),), jnp.float32)
    enc_pos = jnp.clip(jax.random.uniform(part_keys[1], (BLOCKS, 3, PB), jnp.float32, -1.0, 1.0) * steps_of(part_keys[1], (BLOCKS, 3, PB), ((0, 64),), -0.4, 0.0), -1.0, 1.0)
    enc_dest_keys = jax.random.split(jax.random.fold_in(part_keys[2], 1), BLOCKS // BLK_DEV)
    enc_dest_turns = jax.random.permutation(jax.random.fold_in(part_keys[2], 3), BLOCKS // BLK_DEV)
    enc_dest = jax.vmap(lambda own, number: routed_block(jax.random.fold_in(part_keys[2], 2), own, number, BLK_DEV, OWNERS, 1, CAP, 2))(enc_dest_keys, enc_dest_turns).reshape((BLOCKS, 1))
    enc_line = place_ends(jax.random.randint(part_keys[3], (BLOCKS,), 0, LINES_DEV), jax.random.fold_in(part_keys[3], 1), 0, LINES_DEV - 1).astype(jnp.int32)
    dec_pos = jnp.clip(jax.random.uniform(part_keys[4], (BLOCKS, 3, PB), jnp.float32, -1.0, 1.0) * steps_of(part_keys[4], (BLOCKS, 3, PB), ((0, 64),), -0.4, 0.0), -1.0, 1.0)
    dec_dest_keys = jax.random.split(jax.random.fold_in(part_keys[5], 1), BLOCKS // BLK_DEV)
    dec_dest_turns = jax.random.permutation(jax.random.fold_in(part_keys[5], 3), BLOCKS // BLK_DEV)
    dec_dest = jax.vmap(lambda own, number: routed_block(jax.random.fold_in(part_keys[5], 2), own, number, BLK_DEV, OWNERS, 1, CAP, 2))(dec_dest_keys, dec_dest_turns).reshape((BLOCKS, 1))
    dec_line = place_ends(jax.random.randint(part_keys[6], (BLOCKS,), 0, LINES_DEV), jax.random.fold_in(part_keys[6], 1), 0, LINES_DEV - 1).astype(jnp.int32)
    mode_weight = normal_values(key_of[7], (MX, MY, MZ, 2 * C * C), 0.35, 3.0, ((1, 64),))
    skip_weight = normal_values(key_of[8], (C, C), C ** -0.5, 1.0, (), jnp.float32)
    skip_bias = normal_values(key_of[9], (C,), 0.5, 3.0, (), jnp.float32)
    dec_weight = normal_values(key_of[10], (C, C), C ** -0.5, 1.0, (), jnp.float32)
    out_weight = normal_values(key_of[11], (C,), C ** -0.5, 1.0, (), jnp.float32)
    return {"enc_feat": enc_feat, "enc_pos": enc_pos, "enc_dest": enc_dest, "enc_line": enc_line, "dec_pos": dec_pos, "dec_dest": dec_dest, "dec_line": dec_line, "mode_weight": mode_weight, "skip_weight": skip_weight, "skip_bias": skip_bias, "dec_weight": dec_weight, "out_weight": out_weight}


radius_scale = 0.7
spread_cells = 1.5


def kernel_rows(positions):
    planar = positions[:, 0, :] ** 2 + positions[:, 1, :] ** 2
    radial = jnp.exp(-planar / (2.0 * radius_scale ** 2))
    height = (positions[:, 2, :] + 1.0) * (0.5 * (NZ - 1))
    grid_cells = jnp.arange(NZ, dtype=jnp.float32)
    offset = grid_cells[None, None, :] - height[:, :, None]
    return radial[:, :, None] * jnp.exp(-offset * offset / (2.0 * spread_cells ** 2))


def kept_freq(length, kept_count):
    counter = jnp.arange(kept_count, dtype=jnp.int32)
    return jnp.where(counter < kept_count // 2, counter, counter + length - kept_count).astype(jnp.int32)


def decode_blocks(line_data, positions, dec_weight, out_weight):
    kernel = kernel_rows(positions)
    nearby = jnp.einsum('bcz,bpz->bcp', line_data, kernel, precision=lax.Precision.HIGHEST)
    hidden_act = jax.nn.gelu(jnp.einsum('bcp,cd->bdp', nearby, dec_weight, precision=lax.Precision.HIGHEST))
    return jnp.einsum('bdp,d->bp', hidden_act, out_weight, precision=lax.Precision.HIGHEST)


def reference(enc_feat, enc_pos, enc_dest, enc_line, dec_pos, dec_dest, dec_line, mode_weight, skip_weight, skip_bias, dec_weight, out_weight):
    lines_dev = (NX // N_SLAB) * NY

    def encode_blocks(inputs_pair):
        features, positions = inputs_pair
        return jnp.einsum('bcp,bpz->bcz', features, kernel_rows(positions), precision=lax.Precision.HIGHEST)

    terms = lax.map(encode_blocks, (enc_feat.reshape(N_SLAB, BLK_DEV, C, PB), enc_pos.reshape(N_SLAB, BLK_DEV, 3, PB)))
    terms = terms.reshape(BLK_DEV * N_SLAB, C, NZ)
    target = (enc_dest[:, 0] * lines_dev + enc_line).astype(jnp.int32)
    latent = jax.ops.segment_sum(terms, target, num_segments=NX * NY).reshape(NX, NY, C, NZ)

    spectrum = jnp.fft.rfftn(latent, axes=(0, 1, 3))
    kept_x = kept_freq(NX, MX)
    kept_y = kept_freq(NY, MY)
    spectrum = spectrum[kept_x][:, kept_y][:, :, :, :MZ]
    weights = mode_weight.astype(jnp.float32).reshape(MX, MY, MZ, 2, C, C)
    complex_weight = weights[:, :, :, 0] + 1j * weights[:, :, :, 1]
    mixed = jnp.einsum('abck,abkcd->abdk', spectrum, complex_weight, precision=lax.Precision.HIGHEST)
    padded_spectrum = jnp.zeros((NX, NY, C, NZ // 2 + 1), dtype=mixed.dtype)
    padded_spectrum = padded_spectrum.at[kept_x[:, None], kept_y[None, :], :, :MZ].set(mixed)
    spectral = jnp.fft.irfftn(padded_spectrum, s=(NX, NY, NZ), axes=(0, 1, 3))
    skip_term = jnp.einsum('xycz,cd->xydz', latent, skip_weight, precision=lax.Precision.HIGHEST)
    hidden = jax.nn.gelu(spectral + skip_term + skip_bias[None, None, :, None])
    hidden_lines = hidden.reshape(NX * NY, C, NZ)

    source = (dec_dest[:, 0] * lines_dev + dec_line).astype(jnp.int32)

    def decode_group(inputs_pair):
        positions, line_index = inputs_pair
        return decode_blocks(hidden_lines[line_index], positions, dec_weight, out_weight)

    pressure = lax.map(decode_group, (dec_pos.reshape(N_SLAB, BLK_DEV, 3, PB), source.reshape(N_SLAB, BLK_DEV)))
    return pressure.reshape(BLK_DEV * N_SLAB, PB)
```

```python
import functools
import math

import jax
import jax.numpy as jnp
import numpy as np
from jax import lax
from jax.experimental import pallas as pl
from jax.experimental.pallas import tpu as pltpu
from jax.sharding import PartitionSpec as P

C = 32
NX = 128
NY = 128
NZ = 128
MX = 64
MY = 64
MZ = 33
PB = 128
BLK = 128
SLABS = 64
PLANES = NX // SLABS
CAP = 6
SLOTS = SLABS * CAP
LINES = PLANES * NY
MROWS = 40
QROWS = 24
VMEM_LIMIT = 60 * 1024 * 1024

radius_scale = 0.7
spread_cells = 1.5
BF = jnp.bfloat16
F32 = jnp.float32


def split_np(table):
    table = np.asarray(table, np.float32)
    high = table.astype(jnp.bfloat16)
    low = (table - high.astype(np.float32)).astype(jnp.bfloat16)
    return high, low


def split(values):
    high = values.astype(BF)
    low = (values - high.astype(F32)).astype(BF)
    return high, low


def split_table(values):
    high = lax.reduce_precision(values, 8, 7)
    return high.astype(BF), (values - high).astype(BF)


def mm(left, right):
    return jnp.dot(left, right, preferred_element_type=F32)


def mm3(left, right):
    return mm(left[0], right[0]) + (mm(left[1], right[0]) + mm(left[0], right[1]))


def nt(left, right):
    return lax.dot_general(left, right, (((1,), (1,)), ((), ())), preferred_element_type=F32)


def kept(length, count):
    counter = np.arange(count)
    return np.where(counter < count // 2, counter, counter + length - count)


def tables():
    cells = np.arange(NY)
    ky = kept(NY, MY)
    angle = 2.0 * math.pi * ((ky[:, None] * cells[None, :]) % NY) / NY
    cos_y, sin_y = np.cos(angle), np.sin(angle)
    forward_y = np.concatenate([cos_y, -sin_y], axis=0)
    inverse_y = np.concatenate([cos_y.T, sin_y.T], axis=0) / NY
    z_angle = 2.0 * math.pi * ((np.arange(NZ)[:, None] * np.arange(MZ)[None, :]) % NZ) / NZ
    cos_z, sin_z = np.cos(z_angle), np.sin(z_angle)
    forward_z = np.zeros((2 * NZ, 128))
    forward_z[:NZ, :MZ] = cos_z
    forward_z[:NZ, 64 : 64 + MZ] = -sin_z
    forward_z[NZ:, :MZ] = sin_z
    forward_z[NZ:, 64 : 64 + MZ] = cos_z
    weight = np.where(np.arange(MZ) == 0, 1.0, 2.0) / NZ
    inverse_z = np.zeros((2, 2, 64, 2, NZ))
    for twin in range(2):
        inverse_z[0, twin, :MZ, twin, :] = (cos_z * weight[None, :]).T
        inverse_z[1, twin, :MZ, twin, :] = -(sin_z * weight[None, :]).T
    inverse_z = inverse_z.reshape(256, 256)
    kx = kept(NX, MX)
    owner = np.arange(SLABS)
    forward_x, inverse_x = [], []
    for part in (np.cos, np.sin):
        for plane in range(PLANES):
            turns = (kx[:, None] * (PLANES * owner + plane)[None, :]) % NX
            table = part(2.0 * math.pi * turns / NX)
            forward_x.append(table)
            inverse_x.append(table.T / NX)
    forward_x = np.concatenate(forward_x, axis=0)
    inverse_x = np.concatenate(inverse_x, axis=0)
    spread = np.zeros((2, PLANES, C, 2, C, C))
    for channel in range(C):
        for part in range(2):
            spread[part, :, channel, part, channel, :] = 1.0
    spread = spread.reshape(128, 2 * C * C)
    gather = np.zeros((2, 4, C, 2, PLANES, C))
    for channel in range(C):
        for part in range(2):
            gather[part, :, channel, part, :, channel] = 1.0
    gather = gather.reshape(256, 128)
    return (
        split_np(forward_y),
        split_np(inverse_y),
        split_np(forward_z),
        split_np(inverse_z),
        split_np(forward_x),
        split_np(inverse_x),
        np.asarray(spread, jnp.bfloat16),
        np.asarray(gather, jnp.bfloat16),
    )


def params(**extra):
    return pltpu.CompilerParams(vmem_limit_bytes=VMEM_LIMIT, **extra)


def whole(shape):
    return pl.BlockSpec(shape, lambda *_: (0,) * len(shape))


SMEM = pl.BlockSpec(memory_space=pltpu.SMEM)


def routes_kernel(ed_r, ed_c, el_c, dd_r, dd_c, dl_c, out):
    def one(dest_r, dest_c, line_c):
        same = dest_c == dest_r
        rows = lax.broadcasted_iota(jnp.int32, (BLK, BLK), 0)
        cols = lax.broadcasted_iota(jnp.int32, (BLK, BLK), 1)
        before_r = jnp.sum(jnp.where(same & (rows < cols), 1.0, 0.0), axis=0, keepdims=True)
        before_c = jnp.sum(jnp.where(same & (cols < rows), 1.0, 0.0), axis=1, keepdims=True)
        slot_r = dest_r * CAP + before_r.astype(jnp.int32)
        slot_c = dest_c * CAP + before_c.astype(jnp.int32)
        match = slot_c == lax.broadcasted_iota(jnp.int32, (BLK, SLOTS), 1)
        number = lax.broadcasted_iota(jnp.int32, (BLK, SLOTS), 0).astype(F32)
        filled = jnp.sum(jnp.where(match, 1.0, 0.0), axis=0, keepdims=True)
        source = jnp.sum(jnp.where(match, number, 0.0), axis=0, keepdims=True)
        line = jnp.sum(jnp.where(match, line_c.astype(F32), 0.0), axis=0, keepdims=True)
        return slot_r, filled, source.astype(jnp.int32), line.astype(jnp.int32)

    out[...] = jnp.zeros((8, SLOTS), jnp.int32)
    _, filled, source, line = one(ed_r[...], ed_c[...], el_c[...])
    out[0:1, :] = jnp.where(filled > 0.5, source, BLK)
    out[1:2, :] = line
    slot, _, source, line = one(dd_r[...], dd_c[...], dl_c[...])
    out[2:3, :] = source
    out[3:4, :] = line
    out[4:5, 0:BLK] = slot


def encode_kernel(route, feat, pos, out, terms):
    step = pl.program_id(0)

    @pl.when(step == 0)
    def _():
        terms[BLK] = jnp.zeros((C, NZ), F32)

    @pl.when(step < 8)
    def _():
        grid_cells = lax.broadcasted_iota(jnp.int32, (NZ, PB), 0).astype(F32)
        for b in range(16):
            a, o, t = pos[b, 0:1, :], pos[b, 1:2, :], pos[b, 2:3, :]
            radial = jnp.exp((a * a + o * o) * (-1.0 / (2.0 * radius_scale**2)))
            offset = grid_cells - (t + 1.0) * (0.5 * (NZ - 1))
            rows = jnp.exp(offset * offset * (-1.0 / (2.0 * spread_cells**2)))
            fh, fl = split(feat[b] * radial)
            kh, kl = split(rows)
            both = nt(jnp.concatenate([fh, fl], axis=0), kh)
            terms[step * 16 + b] = both[:C] + (both[C:] + nt(fh, kl))

    @pl.when(step >= 8)
    def _():
        base = (step - 8) * 48

        def put(i, carry):
            out[i] = terms[route[0, base + i]]
            return carry

        lax.fori_loop(0, 48, put, 0, unroll=8)


def queries_kernel(route, pos, out):
    lane = lax.broadcasted_iota(jnp.int32, (1, 128), 1)

    def peer(d, carry):
        tags = jnp.zeros((1, 128), F32)
        for r in range(CAP):
            s = d * CAP + r
            out[d, 3 * r : 3 * r + 3, :] = pos[route[2, s]]
            tags = jnp.where(lane == r, route[3, s].astype(F32), tags)
            tags = jnp.where(lane == CAP + r, route[1, s].astype(F32), tags)
        out[d, 18:19, :] = tags
        out[d, 19:24, :] = jnp.zeros((5, 128), F32)
        return carry

    lax.fori_loop(0, SLABS, peer, 0)


def forward_kernel(tags, got, dyh, dyl, zh, zl, latent, message, scratch):
    step = pl.program_id(0)

    @pl.when(step == 0)
    def _():
        latent[...] = jnp.zeros_like(latent)

    for q in range(8):
        for r in range(CAP):
            line = tags[step * 8 + q, CAP + r]
            start = pl.multiple_of(line * C, C)
            latent[pl.ds(start, C), :] += got[q * CAP + r]

    @pl.when(step == 7)
    def _():
        def pair(i, carry):
            plane = i // (C // 2)
            channel = (i % (C // 2)) * 2
            start = plane * NY * C + channel
            first = latent[pl.ds(start, NY, stride=C), :]
            second = latent[pl.ds(start + 1, NY, stride=C), :]
            data = split(jnp.concatenate([first, second], axis=1))
            y = mm3((dyh[...], dyl[...]), data)
            x = jnp.concatenate(
                [
                    jnp.concatenate([y[:MY, :NZ], y[MY:, :NZ]], axis=1),
                    jnp.concatenate([y[:MY, NZ:], y[MY:, NZ:]], axis=1),
                ],
                axis=0,
            )
            s = mm3(split(x), (zh[...], zl[...]))
            at = pl.multiple_of((plane * C + channel) * MY, MY)
            scratch[pl.ds(at, 2 * MY), :] = s
            return carry

        lax.fori_loop(0, PLANES * C // 2, pair, 0, unroll=2)

        def flip(j, carry):
            turned = jnp.transpose(scratch[pl.ds(j, PLANES * C, stride=MY), :])
            message[j, :, 0:64] = turned[:MROWS]
            message[j, :, 64:128] = turned[64 : 64 + MROWS]
            return carry

        lax.fori_loop(0, MY, flip, 0, unroll=2)


def skip_kernel(kh, kl, bias, latent, out):
    data = split(latent[...])
    out[...] = mm3((kh[...], kl[...]), data) + bias[...]


def mix_kernel(spec, weight, xh, xl, spread, gather, ih, il, out):
    step = pl.program_id(0)
    lane = lax.broadcasted_iota(jnp.int32, (64, 128), 1)
    first_plane = (lane & 32) == 0
    real_part = lane < 64
    for sub in range(3):
        kz = step * 3 + sub
        data = split(spec[pl.ds(kz, SLABS, stride=MROWS), :])
        t = mm3((xh[...], xl[...]), data)
        u = jnp.where(first_plane, t[0:64], t[64:128])
        w = pltpu.roll(jnp.where(first_plane, t[128:192], t[192:256]), 64, 1)
        s = u + jnp.where(real_part, w, -w)
        sh, sl = split(s)
        wide = mm(sh, spread[...]) + mm(sl, spread[...])
        acc_re = jnp.zeros((64, 128), F32)
        acc_im = jnp.zeros((64, 128), F32)
        for piece in range(8):
            re = slice(piece * 128, piece * 128 + 128)
            im = slice(C * C + piece * 128, C * C + piece * 128 + 128)
            w_re = weight[sub, :, re].astype(F32)
            w_im = weight[sub, :, im].astype(F32)
            acc_re += wide[:, re] * w_re - wide[:, im] * w_im
            acc_im += wide[:, re] * w_im + wide[:, im] * w_re
        ah, al = split(jnp.concatenate([acc_re, acc_im], axis=1))
        o = mm(ah, gather[...]) + mm(al, gather[...])
        t = mm3((ih[...], il[...]), split(o))
        u = jnp.where(first_plane, t[0:64], t[64:128])
        w = pltpu.roll(jnp.where(first_plane, t[128:192], t[192:256]), 64, 1)
        out[pl.ds(kz, SLABS, stride=MROWS), :] = u + jnp.where(real_part, -w, w)


def decode_kernel(tags, inverse, base, pos, yh, yl, zh, zl, dh, dl, oh, ol, out, modes, hidden):
    lane = lax.broadcasted_iota(jnp.int32, (NY, 128), 1)
    real_part = lane < 64

    def clear(n, carry):
        modes[pl.ds(pl.multiple_of(n * 64 + 32, 32), 32), :] = jnp.zeros((32, 128), F32)
        return carry

    lax.fori_loop(0, NY, clear, 0, unroll=8)

    def planes(k, carry):
        data = split(inverse[pl.ds(k, MY, stride=MROWS), :])
        t = mm3((yh[...], yl[...]), data)
        w = pltpu.roll(t[NY:], 64, 1)
        modes[pl.ds(k, NY, stride=64), :] = t[:NY] + jnp.where(real_part, -w, w)
        return carry

    lax.fori_loop(0, MZ, planes, 0, unroll=3)

    def columns(i, carry):
        turned = jnp.transpose(modes[pl.ds(pl.multiple_of(i * 128, 128), 128), :])
        x = split(jnp.concatenate([turned[:64], turned[64:]], axis=1))
        s = mm3(x, (zh[...], zl[...]))
        for plane in range(PLANES):
            for twin in range(2):
                at = pl.multiple_of((plane * NY + 2 * i + twin) * C, C)
                rows = slice(plane * C, plane * C + C)
                value = s[rows, twin * NZ : twin * NZ + NZ] + base[pl.ds(at, C), :]
                hidden[pl.ds(at, C), :] = jax.nn.gelu(value)
        return carry

    lax.fori_loop(0, NY // 2, columns, 0, unroll=2)

    grid_cells = lax.broadcasted_iota(jnp.int32, (NZ, PB), 0).astype(F32)

    def answer(g, carry):
        near = []
        for i in range(8):
            s = g * 8 + i
            d = s // CAP
            r = s - d * CAP
            line = tags[d, r]
            row = d * QROWS + 3 * r
            a = pos[pl.ds(row, 1), :]
            o = pos[pl.ds(row + 1, 1), :]
            t = pos[pl.ds(row + 2, 1), :]
            radial = jnp.exp((a * a + o * o) * (-1.0 / (2.0 * radius_scale**2)))
            offset = grid_cells - (t + 1.0) * (0.5 * (NZ - 1))
            rows = jnp.exp(offset * offset * (-1.0 / (2.0 * spread_cells**2)))
            kh, kl = split(rows)
            hh, hl = split(hidden[pl.ds(pl.multiple_of(line * C, C), C), :])
            both = mm(jnp.concatenate([hh, hl], axis=0), kh)
            near.append((both[:C] + (both[C:] + mm(hh, kl))) * radial)
        nearby = split(jnp.concatenate(near, axis=0))
        act = split(jax.nn.gelu(mm3((dh[...], dl[...]), nearby)))
        out[pl.ds(pl.multiple_of(g * 8, 8), 8), :] = mm3((oh[...], ol[...]), act)
        return carry

    lax.fori_loop(0, SLOTS // 8, answer, 0)


def local(
    enc_feat,
    enc_pos,
    enc_dest,
    enc_line,
    dec_pos,
    dec_dest,
    dec_line,
    mode_weight,
    skip_weight,
    skip_bias,
    dec_weight,
    out_weight,
):
    forward_y, inverse_y, forward_z, inverse_z, forward_x, inverse_x, spread, gather = tables()
    exchange = functools.partial(
        lax.all_to_all, axis_name="slab", split_axis=0, concat_axis=0, tiled=True
    )
    route = pl.pallas_call(
        routes_kernel, out_shape=jax.ShapeDtypeStruct((8, SLOTS), jnp.int32), name="routes"
    )(
        enc_dest.reshape(1, BLK),
        enc_dest,
        enc_line.reshape(BLK, 1),
        dec_dest.reshape(1, BLK),
        dec_dest,
        dec_line.reshape(BLK, 1),
    )
    queries = pl.pallas_call(
        queries_kernel,
        out_shape=jax.ShapeDtypeStruct((SLABS, QROWS, 128), F32),
        in_specs=[SMEM, whole((BLK, 3, PB))],
        out_specs=whole((SLABS, QROWS, 128)),
        name="queries",
    )(route, dec_pos)
    packed = pl.pallas_call(
        encode_kernel,
        out_shape=jax.ShapeDtypeStruct((SLOTS, C, NZ), F32),
        grid=(16,),
        in_specs=[
            SMEM,
            pl.BlockSpec((16, C, PB), lambda i: (jnp.minimum(i, 7), 0, 0)),
            pl.BlockSpec((16, 3, PB), lambda i: (jnp.minimum(i, 7), 0, 0)),
        ],
        out_specs=pl.BlockSpec((48, C, NZ), lambda i: (jnp.maximum(i - 8, 0), 0, 0)),
        scratch_shapes=[pltpu.VMEM((BLK + 1, C, NZ), F32)],
        compiler_params=params(),
        name="encode",
    )(route, enc_feat, enc_pos)
    got_queries = exchange(queries)
    got_terms = exchange(packed)
    tags = got_queries[:, 18, 0 : 2 * CAP].astype(jnp.int32)
    latent, message = pl.pallas_call(
        forward_kernel,
        out_shape=(
            jax.ShapeDtypeStruct((LINES * C, NZ), F32),
            jax.ShapeDtypeStruct((MY, MROWS, 128), F32),
        ),
        grid=(8,),
        in_specs=[
            SMEM,
            pl.BlockSpec((48, C, NZ), lambda i: (i, 0, 0)),
            whole((2 * MY, NY)),
            whole((2 * MY, NY)),
            whole((2 * NZ, 128)),
            whole((2 * NZ, 128)),
        ],
        out_specs=(whole((LINES * C, NZ)), whole((MY, MROWS, 128))),
        scratch_shapes=[pltpu.VMEM((PLANES * C * MY, 128), F32)],
        compiler_params=params(),
        name="forward",
    )(tags, got_terms, *forward_y, *forward_z)
    spectrum = exchange(message)
    skip_wide = jnp.kron(jnp.eye(8, dtype=F32), skip_weight.T)
    base = pl.pallas_call(
        skip_kernel,
        out_shape=jax.ShapeDtypeStruct((LINES * C, NZ), F32),
        grid=(32,),
        in_specs=[
            whole((256, 256)),
            whole((256, 256)),
            whole((256, 1)),
            pl.BlockSpec((256, NZ), lambda i: (i, 0)),
        ],
        out_specs=pl.BlockSpec((256, NZ), lambda i: (i, 0)),
        compiler_params=params(),
        name="skip",
    )(*split_table(skip_wide), jnp.tile(skip_bias, 8)[:, None], latent)
    weight = jnp.transpose(mode_weight.reshape(MX, MZ, 2 * C * C), (1, 0, 2))
    mixed = pl.pallas_call(
        mix_kernel,
        out_shape=jax.ShapeDtypeStruct((SLABS * MROWS, 128), F32),
        grid=(11,),
        in_specs=[
            whole((SLABS * MROWS, 128)),
            pl.BlockSpec((3, MX, 2 * C * C), lambda i: (i, 0, 0)),
            whole((256, 64)),
            whole((256, 64)),
            whole((128, 2 * C * C)),
            whole((256, 128)),
            whole((256, 64)),
            whole((256, 64)),
        ],
        out_specs=whole((SLABS * MROWS, 128)),
        compiler_params=params(),
        name="mix",
    )(spectrum.reshape(SLABS * MROWS, 128), weight, *forward_x, spread, gather, *inverse_x)
    inverse = exchange(mixed.reshape(SLABS, MROWS, 128))
    dec_wide = jnp.kron(jnp.eye(8, dtype=F32), dec_weight.T)
    out_wide = jnp.kron(jnp.eye(8, dtype=F32), out_weight[None, :])
    vm = pl.BlockSpec(memory_space=pltpu.VMEM)
    answers = pl.pallas_call(
        decode_kernel,
        out_shape=jax.ShapeDtypeStruct((SLOTS, PB), F32),
        in_specs=[SMEM] + [vm] * 11,
        out_specs=vm,
        scratch_shapes=[
            pltpu.VMEM((NY * 64, 128), F32),
            pltpu.VMEM((LINES * C, NZ), F32),
        ],
        compiler_params=params(),
        name="decode",
    )(
        tags,
        inverse.reshape(MY * MROWS, 128),
        base,
        got_queries.reshape(SLABS * QROWS, 128),
        *inverse_y,
        *inverse_z,
        *split_table(dec_wide),
        *split_table(out_wide),
    )
    returned = exchange(answers)
    return returned[route[4, 0:BLK]]


def solution(mesh):
    placed = (
        P(("geo", "slab"), None, None),
        P(("geo", "slab"), None, None),
        P(("geo", "slab"), None),
        P(("geo", "slab")),
        P(("geo", "slab"), None, None),
        P(("geo", "slab"), None),
        P(("geo", "slab")),
        P(None, "slab", None, None),
        P(),
        P(),
        P(),
        P(),
    )
    return jax.shard_map(
        local, mesh=mesh, in_specs=placed, out_specs=P(("geo", "slab"), None), check_vma=False
    )
```

```python
import functools
import math

import jax
import jax.numpy as jnp
import numpy as np
from jax import lax
from jax.experimental import pallas as pl
from jax.experimental.pallas import tpu as pltpu
from jax.sharding import PartitionSpec as P

C = 32
NX = 128
NY = 128
NZ = 128
MX = 64
MY = 64
MZ = 33
PB = 128
BLK = 128
SLABS = 64
PLANES = NX // SLABS
CAP = 6
SLOTS = SLABS * CAP
LINES = PLANES * NY
MROWS = 40
QROWS = 24
VMEM_LIMIT = 60 * 1024 * 1024

radius_scale = 0.7
spread_cells = 1.5
BF = jnp.bfloat16
F32 = jnp.float32


def split_np(table):
    table = np.asarray(table, np.float32)
    high = table.astype(jnp.bfloat16)
    low = (table - high.astype(np.float32)).astype(jnp.bfloat16)
    return high, low


def left_np(table):
    high, low = split_np(table)
    return np.concatenate([high, low, high], axis=1)


def right_np(table):
    high, low = split_np(table)
    return np.concatenate([high, high, low], axis=0)


def split(values):
    high = values.astype(BF)
    low = (values - high.astype(F32)).astype(BF)
    return high, low


def left_table(values):
    high = lax.reduce_precision(values, 8, 7)
    low = (values - high).astype(BF)
    high = high.astype(BF)
    return jnp.concatenate([high, low, high], axis=1)


def left3(values):
    high, low = split(values)
    return jnp.concatenate([high, low, high], axis=1)


def right3(values):
    high, low = split(values)
    return jnp.concatenate([high, high, low], axis=0)


def mm(left, right):
    return jnp.dot(left, right, preferred_element_type=F32)


def nt(left, right):
    return lax.dot_general(left, right, (((1,), (1,)), ((), ())), preferred_element_type=F32)


def kept(length, count):
    counter = np.arange(count)
    return np.where(counter < count // 2, counter, counter + length - count)


def tables():
    cells = np.arange(NY)
    ky = kept(NY, MY)
    angle = 2.0 * math.pi * ((ky[:, None] * cells[None, :]) % NY) / NY
    cos_y, sin_y = np.cos(angle), np.sin(angle)
    forward_y = np.concatenate([cos_y, -sin_y], axis=0)
    inverse_y = np.concatenate([cos_y.T, sin_y.T], axis=0) / NY
    z_angle = 2.0 * math.pi * ((np.arange(NZ)[:, None] * np.arange(MZ)[None, :]) % NZ) / NZ
    cos_z, sin_z = np.cos(z_angle), np.sin(z_angle)
    forward_z = np.zeros((2 * NZ, 128))
    forward_z[:NZ, :MZ] = cos_z
    forward_z[:NZ, 64 : 64 + MZ] = -sin_z
    forward_z[NZ:, :MZ] = sin_z
    forward_z[NZ:, 64 : 64 + MZ] = cos_z
    weight = np.where(np.arange(MZ) == 0, 1.0, 2.0) / NZ
    inverse_z = np.zeros((2, 2, 64, 2, NZ))
    for twin in range(2):
        inverse_z[0, twin, :MZ, twin, :] = (cos_z * weight[None, :]).T
        inverse_z[1, twin, :MZ, twin, :] = -(sin_z * weight[None, :]).T
    inverse_z = inverse_z.reshape(256, 256)
    kx = kept(NX, MX)
    owner = np.arange(SLABS)
    forward_x, inverse_x = [], []
    for part in (np.cos, np.sin):
        for plane in range(PLANES):
            turns = (kx[:, None] * (PLANES * owner + plane)[None, :]) % NX
            table = part(2.0 * math.pi * turns / NX)
            forward_x.append(table)
            inverse_x.append(table.T / NX)
    forward_x = np.concatenate(forward_x, axis=0)
    inverse_x = np.concatenate(inverse_x, axis=0)
    spread = np.zeros((2, PLANES, C, 2, C, C))
    for channel in range(C):
        for part in range(2):
            spread[part, :, channel, part, channel, :] = 1.0
    spread = spread.reshape(128, 2 * C * C)
    gather = np.zeros((2, 4, C, 2, PLANES, C))
    for channel in range(C):
        for part in range(2):
            gather[part, :, channel, part, :, channel] = 1.0
    gather = gather.reshape(256, 128)
    return (
        left_np(forward_y),
        left_np(inverse_y),
        right_np(forward_z),
        right_np(inverse_z),
        left_np(forward_x),
        left_np(inverse_x),
        np.asarray(np.concatenate([spread, spread], axis=0), jnp.bfloat16),
        np.asarray(np.concatenate([gather, gather], axis=0), jnp.bfloat16),
    )


def params(**extra):
    return pltpu.CompilerParams(vmem_limit_bytes=VMEM_LIMIT, **extra)


def cost(microseconds):
    return pl.CostEstimate(
        flops=0, transcendentals=0, bytes_accessed=int(microseconds * 2_000_000)
    )


def whole(shape):
    return pl.BlockSpec(shape, lambda *_: (0,) * len(shape))


SMEM = pl.BlockSpec(memory_space=pltpu.SMEM)


def routes_kernel(ed, el, dd, dl, out):
    rows = lax.broadcasted_iota(jnp.int32, (BLK, BLK), 0)
    cols = lax.broadcasted_iota(jnp.int32, (BLK, BLK), 1)

    def column(row):
        spread_row = jnp.broadcast_to(row.astype(F32), (BLK, BLK))
        return jnp.sum(jnp.where(rows == cols, spread_row, 0.0), axis=1, keepdims=True)

    def one(dest_r, line_r):
        dest_c = column(dest_r).astype(jnp.int32)
        line_c = column(line_r)
        same = dest_c == dest_r
        before_r = jnp.sum(jnp.where(same & (rows < cols), 1.0, 0.0), axis=0, keepdims=True)
        slot_r = dest_r * CAP + before_r.astype(jnp.int32)
        slot_c = column(slot_r).astype(jnp.int32)
        match = slot_c == lax.broadcasted_iota(jnp.int32, (BLK, SLOTS), 1)
        number = lax.broadcasted_iota(jnp.int32, (BLK, SLOTS), 0).astype(F32)
        filled = jnp.sum(jnp.where(match, 1.0, 0.0), axis=0, keepdims=True)
        source = jnp.sum(jnp.where(match, number, 0.0), axis=0, keepdims=True)
        line = jnp.sum(jnp.where(match, line_c, 0.0), axis=0, keepdims=True)
        return slot_r, filled, source.astype(jnp.int32), line.astype(jnp.int32)

    out[...] = jnp.zeros((8, SLOTS), jnp.int32)
    _, filled, source, line = one(ed[...], el[...])
    out[0:1, :] = jnp.where(filled > 0.5, source, BLK)
    out[1:2, :] = line
    slot, _, source, line = one(dd[...], dl[...])
    out[2:3, :] = source
    out[3:4, :] = line
    out[4:5, 0:BLK] = slot


def encode_kernel(route, feat, pos, out, terms):
    step = pl.program_id(0)

    @pl.when(step == 0)
    def _():
        terms[BLK] = jnp.zeros((C, NZ), F32)

    @pl.when(step < 8)
    def _():
        grid_cells = lax.broadcasted_iota(jnp.int32, (NZ, PB), 0).astype(F32)
        for b in range(16):
            a, o, t = pos[0, b : b + 1, :], pos[1, b : b + 1, :], pos[2, b : b + 1, :]
            radial = jnp.exp((a * a + o * o) * (-1.0 / (2.0 * radius_scale**2)))
            offset = grid_cells - (t + 1.0) * (0.5 * (NZ - 1))
            rows = jnp.exp(offset * offset * (-1.0 / (2.0 * spread_cells**2)))
            fh, fl = split(feat[b] * radial)
            kh, kl = split(rows)
            both = nt(jnp.concatenate([fh, fl], axis=0), kh)
            terms[step * 16 + b] = both[:C] + (both[C:] + nt(fh, kl))

    @pl.when(step >= 8)
    def _():
        base = (step - 8) * 48

        def put(i, carry):
            out[i] = terms[route[0, base + i]]
            return carry

        lax.fori_loop(0, 48, put, 0, unroll=8)


def queries_kernel(route, pos, out):
    lane = lax.broadcasted_iota(jnp.int32, (1, 128), 1)

    def peer(d, carry):
        tags = jnp.zeros((1, 128), F32)
        for r in range(CAP):
            s = d * CAP + r
            for part in range(3):
                out[d, 3 * r + part : 3 * r + part + 1, :] = pos[part, pl.ds(route[2, s], 1), :]
            tags = jnp.where(lane == r, route[3, s].astype(F32), tags)
            tags = jnp.where(lane == CAP + r, route[1, s].astype(F32), tags)
        out[d, 18:19, :] = tags
        out[d, 19:24, :] = jnp.zeros((5, 128), F32)
        return carry

    lax.fori_loop(0, SLABS, peer, 0)


def profile_kernel(pos, out):
    step = pl.program_id(0)
    grid_cells = lax.broadcasted_iota(jnp.int32, (NZ, PB), 0).astype(F32)

    def one(d, carry):
        for r in range(CAP):
            a = pos[d, 3 * r : 3 * r + 1, :]
            o = pos[d, 3 * r + 1 : 3 * r + 2, :]
            t = pos[d, 3 * r + 2 : 3 * r + 3, :]
            radial = jnp.exp((a * a + o * o) * (-1.0 / (2.0 * radius_scale**2)))
            offset = grid_cells - (t + 1.0) * (0.5 * (NZ - 1))
            rows = jnp.exp(offset * offset * (-1.0 / (2.0 * spread_cells**2))) * radial
            kh, kl = split(rows)
            out[d * CAP + r, :, 0:PB] = kh
            out[d * CAP + r, :, PB : 2 * PB] = kl
        return carry

    lax.fori_loop(0, 4, one, 0)


def forward_kernel(tags, got, dy, fz, latent, message, scratch):
    step = pl.program_id(0)

    @pl.when(step == 0)
    def _():
        latent[...] = jnp.zeros_like(latent)

    for q in range(8):
        for r in range(CAP):
            line = tags[step * 8 + q, CAP + r]
            start = pl.multiple_of(line * C, C)
            latent[pl.ds(start, C), :] += got[q * CAP + r]

    @pl.when(step == 7)
    def _():
        def quad(i, carry):
            plane = i // (C // 4)
            channel = (i % (C // 4)) * 4
            start = plane * NY * C + channel
            data = jnp.concatenate(
                [latent[pl.ds(start + n, NY, stride=C), :] for n in range(4)], axis=1
            )
            y = mm(dy[...], right3(data))
            x = jnp.concatenate(
                [
                    jnp.concatenate(
                        [y[:MY, n * NZ : n * NZ + NZ], y[MY:, n * NZ : n * NZ + NZ]], axis=1
                    )
                    for n in range(4)
                ],
                axis=0,
            )
            at = pl.multiple_of((plane * C + channel) * MY, MY)
            scratch[pl.ds(at, 4 * MY), :] = mm(left3(x), fz[...])
            return carry

        lax.fori_loop(0, PLANES * C // 4, quad, 0, unroll=2)

        def flip(j, carry):
            turned = jnp.transpose(scratch[pl.ds(j, PLANES * C, stride=MY), :])
            message[j, :, 0:64] = turned[:MROWS]
            message[j, :, 64:128] = turned[64 : 64 + MROWS]
            return carry

        lax.fori_loop(0, MY, flip, 0, unroll=4)


def skip_kernel(kron, bias, latent, out):
    for n in range(4):
        rows = slice(n * 256, n * 256 + 256)
        out[rows, :] = mm(kron[...], right3(latent[rows, :])) + bias[...]


def planes_of(t, first_plane):
    u = jnp.where(first_plane, t[0:64], t[64:128])
    w = jnp.where(first_plane, t[128:192], t[192:256])
    return u, pltpu.roll(w, 64, 1)


def mix_kernel(spec, weight, fx, spread, gather, ix, out):
    step = pl.program_id(0)
    lane = lax.broadcasted_iota(jnp.int32, (64, 128), 1)
    first_plane = (lane & 32) == 0
    real_part = lane < 64
    data = jnp.concatenate(
        [spec[pl.ds(step * 3 + n, SLABS, stride=MROWS), :] for n in range(3)], axis=1
    )
    t = mm(fx[...], right3(data))
    rows = []
    for n in range(3):
        u, w = planes_of(t[:, n * 128 : n * 128 + 128], first_plane)
        rows.append(u + jnp.where(real_part, w, -w))
    sh, sl = split(jnp.concatenate(rows, axis=0))
    wide = mm(jnp.concatenate([sh, sl], axis=1), spread[...])
    rows = []
    for n in range(3):
        acc_re = jnp.zeros((64, 128), F32)
        acc_im = jnp.zeros((64, 128), F32)
        part = slice(n * 64, n * 64 + 64)
        for piece in range(8):
            re = slice(piece * 128, piece * 128 + 128)
            im = slice(C * C + piece * 128, C * C + piece * 128 + 128)
            w_re = weight[n, :, re].astype(F32)
            w_im = weight[n, :, im].astype(F32)
            acc_re += wide[part, re] * w_re - wide[part, im] * w_im
            acc_im += wide[part, re] * w_im + wide[part, im] * w_re
        rows.append(jnp.concatenate([acc_re, acc_im], axis=1))
    ah, al = split(jnp.concatenate(rows, axis=0))
    o = mm(jnp.concatenate([ah, al], axis=1), gather[...])
    data = jnp.concatenate([o[n * 64 : n * 64 + 64] for n in range(3)], axis=1)
    t = mm(ix[...], right3(data))
    for n in range(3):
        u, w = planes_of(t[:, n * 128 : n * 128 + 128], first_plane)
        out[pl.ds(step * 3 + n, SLABS, stride=MROWS), :] = u + jnp.where(real_part, -w, w)


def decode_kernel(tags, inverse, base, profile, iy, iz, dw, ow, out, modes, hidden):
    step = pl.program_id(0)

    @pl.when(step == 0)
    def _():
        lane = lax.broadcasted_iota(jnp.int32, (NY, 128), 1)
        real_part = lane < 64

        def clear(n, carry):
            modes[pl.ds(pl.multiple_of(n * 64 + 32, 32), 32), :] = jnp.zeros((32, 128), F32)
            return carry

        lax.fori_loop(0, NY, clear, 0, unroll=8)

        def planes(i, carry):
            data = jnp.concatenate(
                [inverse[pl.ds(i * 3 + n, MY, stride=MROWS), :] for n in range(3)], axis=1
            )
            t = mm(iy[...], right3(data))
            for n in range(3):
                cols = slice(n * 128, n * 128 + 128)
                w = pltpu.roll(t[NY:, cols], 64, 1)
                modes[pl.ds(i * 3 + n, NY, stride=64), :] = t[:NY, cols] + jnp.where(
                    real_part, -w, w
                )
            return carry

        lax.fori_loop(0, MZ // 3, planes, 0)

        def columns(i, carry):
            rows = []
            for n in range(4):
                at = pl.multiple_of((i * 4 + n) * 128, 128)
                turned = jnp.transpose(modes[pl.ds(at, 128), :])
                rows.append(jnp.concatenate([turned[:64], turned[64:]], axis=1))
            s = mm(left3(jnp.concatenate(rows, axis=0)), iz[...])
            for n in range(4):
                for plane in range(PLANES):
                    for twin in range(2):
                        at = pl.multiple_of((plane * NY + 2 * (i * 4 + n) + twin) * C, C)
                        top = n * 64 + plane * C
                        value = s[top : top + C, twin * NZ : twin * NZ + NZ] + base[pl.ds(at, C), :]
                        hidden[pl.ds(at, C), :] = jax.nn.gelu(value)
            return carry

        lax.fori_loop(0, NY // 8, columns, 0)

    for pair in range(2):
        sides = []
        for half in range(2):
            near = []
            for i in range(6):
                q = (pair * 2 + half) * 6 + i
                line = tags[step * 4 + pair * 2 + half, i]
                hh, hl = split(hidden[pl.ds(pl.multiple_of(line * C, C), C), :])
                both = mm(jnp.concatenate([hh, hl], axis=0), profile[q])
                near.append(both[:C, :PB] + (both[C:, :PB] + both[:C, PB:]))
            sides.append(jnp.concatenate(near, axis=0))
        act = jax.nn.gelu(mm(dw[...], right3(jnp.concatenate(sides, axis=1))))
        result = mm(ow[...], right3(act))
        for half in range(2):
            d = pair * 2 + half
            out[d] = result[:, half * PB : half * PB + PB]


def local(
    enc_feat,
    enc_pos,
    enc_dest,
    enc_line,
    dec_pos,
    dec_dest,
    dec_line,
    mode_weight,
    skip_weight,
    skip_bias,
    dec_weight,
    out_weight,
):
    forward_y, inverse_y, forward_z, inverse_z, forward_x, inverse_x, spread, gather = tables()
    exchange = functools.partial(
        lax.all_to_all, axis_name="slab", split_axis=0, concat_axis=0, tiled=True
    )
    route = pl.pallas_call(
        routes_kernel, out_shape=jax.ShapeDtypeStruct((8, SLOTS), jnp.int32), name="routes"
    )(
        enc_dest.reshape(1, BLK),
        enc_line.reshape(1, BLK),
        dec_dest.reshape(1, BLK),
        dec_line.reshape(1, BLK),
    )
    queries = pl.pallas_call(
        queries_kernel,
        out_shape=jax.ShapeDtypeStruct((SLABS, QROWS, 128), F32),
        in_specs=[SMEM, whole((3, BLK, PB))],
        out_specs=whole((SLABS, QROWS, 128)),
        name="queries",
    )(route, jnp.transpose(dec_pos, (1, 0, 2)))
    packed = pl.pallas_call(
        encode_kernel,
        out_shape=jax.ShapeDtypeStruct((SLOTS, C, NZ), F32),
        grid=(16,),
        in_specs=[
            SMEM,
            pl.BlockSpec((16, C, PB), lambda i: (jnp.minimum(i, 7), 0, 0)),
            pl.BlockSpec((3, 16, PB), lambda i: (0, jnp.minimum(i, 7), 0)),
        ],
        out_specs=pl.BlockSpec((48, C, NZ), lambda i: (jnp.maximum(i - 8, 0), 0, 0)),
        scratch_shapes=[pltpu.VMEM((BLK + 1, C, NZ), F32)],
        compiler_params=params(),
        cost_estimate=cost(12),
        name="encode",
    )(route, enc_feat, jnp.transpose(enc_pos, (1, 0, 2)))
    got_queries = exchange(queries)
    got_terms = exchange(packed)
    tags = got_queries[:, 18, 0 : 2 * CAP].astype(jnp.int32)
    profile = pl.pallas_call(
        profile_kernel,
        out_shape=jax.ShapeDtypeStruct((SLOTS, NZ, 2 * PB), BF),
        grid=(16,),
        in_specs=[pl.BlockSpec((4, QROWS, PB), lambda i: (i, 0, 0))],
        out_specs=pl.BlockSpec((24, NZ, 2 * PB), lambda i: (i, 0, 0)),
        compiler_params=params(),
        cost_estimate=cost(25),
        name="profile",
    )(got_queries)
    skip_wide = left_table(jnp.kron(jnp.eye(8, dtype=F32), skip_weight.T))
    skip_bias_wide = jnp.tile(skip_bias, 8)[:, None]
    dec_wide = left_table(jnp.kron(jnp.eye(CAP, dtype=F32), dec_weight.T))
    out_wide = left_table(jnp.kron(jnp.eye(CAP, dtype=F32), out_weight[None, :]))
    latent, message = pl.pallas_call(
        forward_kernel,
        out_shape=(
            jax.ShapeDtypeStruct((LINES * C, NZ), F32),
            jax.ShapeDtypeStruct((MY, MROWS, 128), F32),
        ),
        grid=(8,),
        in_specs=[
            SMEM,
            pl.BlockSpec((48, C, NZ), lambda i: (i, 0, 0)),
            whole((2 * MY, 3 * NY)),
            whole((6 * NZ, 128)),
        ],
        out_specs=(whole((LINES * C, NZ)), whole((MY, MROWS, 128))),
        scratch_shapes=[pltpu.VMEM((PLANES * C * MY, 128), F32)],
        compiler_params=params(),
        name="forward",
    )(tags, got_terms, forward_y, forward_z)
    spectrum = exchange(message)
    base = pl.pallas_call(
        skip_kernel,
        out_shape=jax.ShapeDtypeStruct((LINES * C, NZ), F32),
        grid=(8,),
        in_specs=[
            whole((256, 768)),
            whole((256, 1)),
            pl.BlockSpec((1024, NZ), lambda i: (i, 0)),
        ],
        out_specs=pl.BlockSpec((1024, NZ), lambda i: (i, 0)),
        compiler_params=params(),
        cost_estimate=cost(12),
        name="skip",
    )(skip_wide, skip_bias_wide, latent)
    weight = jnp.transpose(mode_weight.reshape(MX, MZ, 2 * C * C), (1, 0, 2))
    mixed = pl.pallas_call(
        mix_kernel,
        out_shape=jax.ShapeDtypeStruct((SLABS * MROWS, 128), F32),
        grid=(11,),
        in_specs=[
            whole((SLABS * MROWS, 128)),
            pl.BlockSpec((3, MX, 2 * C * C), lambda i: (i, 0, 0)),
            whole((256, 192)),
            whole((256, 2 * C * C)),
            whole((512, 128)),
            whole((256, 192)),
        ],
        out_specs=whole((SLABS * MROWS, 128)),
        compiler_params=params(),
        name="mix",
    )(spectrum.reshape(SLABS * MROWS, 128), weight, forward_x, spread, gather, inverse_x)
    inverse = exchange(mixed.reshape(SLABS, MROWS, 128))
    answers = pl.pallas_call(
        decode_kernel,
        out_shape=jax.ShapeDtypeStruct((SLABS, CAP, PB), F32),
        grid=(16,),
        in_specs=[
            SMEM,
            whole((MY * MROWS, 128)),
            whole((LINES * C, NZ)),
            pl.BlockSpec((24, NZ, 2 * PB), lambda i: (i, 0, 0)),
            whole((2 * NY, 192)),
            whole((768, 2 * NZ)),
            whole((CAP * C, 3 * CAP * C)),
            whole((CAP, 3 * CAP * C)),
        ],
        out_specs=pl.BlockSpec((4, CAP, PB), lambda i: (i, 0, 0)),
        scratch_shapes=[
            pltpu.VMEM((NY * 64, 128), F32),
            pltpu.VMEM((LINES * C, NZ), F32),
        ],
        compiler_params=params(),
        name="decode",
    )(
        tags,
        inverse.reshape(MY * MROWS, 128),
        base,
        profile,
        inverse_y,
        inverse_z,
        dec_wide,
        out_wide,
    )
    returned = exchange(answers)
    slot = route[4, 0:BLK]
    return returned[slot // CAP, slot % CAP]


def solution(mesh):
    placed = (
        P(("geo", "slab"), None, None),
        P(("geo", "slab"), None, None),
        P(("geo", "slab"), None),
        P(("geo", "slab")),
        P(("geo", "slab"), None, None),
        P(("geo", "slab"), None),
        P(("geo", "slab")),
        P(None, "slab", None, None),
        P(),
        P(),
        P(),
        P(),
    )
    return jax.shard_map(
        local, mesh=mesh, in_specs=placed, out_specs=P(("geo", "slab"), None), check_vma=False
    )
```

```python
import functools
import math

import jax
import jax.numpy as jnp
import numpy as np
from jax import lax
from jax.experimental import pallas as pl
from jax.experimental.pallas import tpu as pltpu
from jax.sharding import PartitionSpec as P

C = 32
NX = 128
NY = 128
NZ = 128
MX = 64
MY = 64
MZ = 33
PB = 128
BLK = 128
SLABS = 64
PLANES = NX // SLABS
CAP = 6
SLOTS = SLABS * CAP
LINES = PLANES * NY
MROWS = 40
QROWS = 24
VMEM_LIMIT = 60 * 1024 * 1024

radius_scale = 0.7
spread_cells = 1.5
BF = jnp.bfloat16
F32 = jnp.float32


def split_np(table):
    table = np.asarray(table, np.float32)
    high = table.astype(jnp.bfloat16)
    low = (table - high.astype(np.float32)).astype(jnp.bfloat16)
    return high, low


def left_np(table):
    high, low = split_np(table)
    return np.concatenate([high, low, high], axis=1)


def right_np(table):
    high, low = split_np(table)
    return np.concatenate([high, high, low], axis=0)


def split(values):
    high = values.astype(BF)
    low = (values - high.astype(F32)).astype(BF)
    return high, low


def left_table(values):
    high = lax.reduce_precision(values, 8, 7)
    low = (values - high).astype(BF)
    high = high.astype(BF)
    return jnp.concatenate([high, low, high], axis=1)


def left3(values):
    high, low = split(values)
    return jnp.concatenate([high, low, high], axis=1)


def right3(values):
    high, low = split(values)
    return jnp.concatenate([high, high, low], axis=0)


def mm(left, right):
    return jnp.dot(left, right, preferred_element_type=F32)


def nt(left, right):
    return lax.dot_general(left, right, (((1,), (1,)), ((), ())), preferred_element_type=F32)


def kept(length, count):
    counter = np.arange(count)
    return np.where(counter < count // 2, counter, counter + length - count)


def tables():
    cells = np.arange(NY)
    ky = kept(NY, MY)
    angle = 2.0 * math.pi * ((ky[:, None] * cells[None, :]) % NY) / NY
    cos_y, sin_y = np.cos(angle), np.sin(angle)
    forward_y = np.concatenate([cos_y, -sin_y], axis=0)
    inverse_y = np.concatenate([cos_y.T, sin_y.T], axis=0) / NY
    z_angle = 2.0 * math.pi * ((np.arange(NZ)[:, None] * np.arange(MZ)[None, :]) % NZ) / NZ
    cos_z, sin_z = np.cos(z_angle), np.sin(z_angle)
    forward_z = np.zeros((2 * NZ, 128))
    forward_z[:NZ, :MZ] = cos_z
    forward_z[:NZ, 64 : 64 + MZ] = -sin_z
    forward_z[NZ:, :MZ] = sin_z
    forward_z[NZ:, 64 : 64 + MZ] = cos_z
    weight = np.where(np.arange(MZ) == 0, 1.0, 2.0) / NZ
    inverse_z = np.zeros((2, 2, 64, 2, NZ))
    for twin in range(2):
        inverse_z[0, twin, :MZ, twin, :] = (cos_z * weight[None, :]).T
        inverse_z[1, twin, :MZ, twin, :] = -(sin_z * weight[None, :]).T
    inverse_z = inverse_z.reshape(256, 256)
    kx = kept(NX, MX)
    owner = np.arange(SLABS)
    forward_x, inverse_x = [], []
    for part in (np.cos, np.sin):
        for plane in range(PLANES):
            turns = (kx[:, None] * (PLANES * owner + plane)[None, :]) % NX
            table = part(2.0 * math.pi * turns / NX)
            forward_x.append(table)
            inverse_x.append(table.T / NX)
    forward_x = np.concatenate(forward_x, axis=0)
    inverse_x = np.concatenate(inverse_x, axis=0)
    spread = np.zeros((2, PLANES, C, 2, C, C))
    for channel in range(C):
        for part in range(2):
            spread[part, :, channel, part, channel, :] = 1.0
    spread = spread.reshape(128, 2 * C * C)
    gather = np.zeros((2, 4, C, 2, PLANES, C))
    for channel in range(C):
        for part in range(2):
            gather[part, :, channel, part, :, channel] = 1.0
    gather = gather.reshape(256, 128)
    return (
        left_np(forward_y),
        left_np(inverse_y),
        right_np(forward_z),
        right_np(inverse_z),
        left_np(forward_x),
        left_np(inverse_x),
        np.asarray(np.concatenate([spread, spread], axis=0), jnp.bfloat16),
        np.asarray(np.concatenate([gather, gather], axis=0), jnp.bfloat16),
    )


def params(**extra):
    return pltpu.CompilerParams(vmem_limit_bytes=VMEM_LIMIT, **extra)


def cost(microseconds):
    return pl.CostEstimate(
        flops=0, transcendentals=0, bytes_accessed=int(microseconds * 2_000_000)
    )


def whole(shape):
    return pl.BlockSpec(shape, lambda *_: (0,) * len(shape))


SMEM = pl.BlockSpec(memory_space=pltpu.SMEM)


def routes_kernel(ed, el, dd, dl, out):
    rows = lax.broadcasted_iota(jnp.int32, (BLK, BLK), 0)
    cols = lax.broadcasted_iota(jnp.int32, (BLK, BLK), 1)

    def column(row):
        spread_row = jnp.broadcast_to(row.astype(F32), (BLK, BLK))
        return jnp.sum(jnp.where(rows == cols, spread_row, 0.0), axis=1, keepdims=True)

    def one(dest_r, line_r):
        dest_c = column(dest_r).astype(jnp.int32)
        line_c = column(line_r)
        same = dest_c == dest_r
        before_r = jnp.sum(jnp.where(same & (rows < cols), 1.0, 0.0), axis=0, keepdims=True)
        slot_r = dest_r * CAP + before_r.astype(jnp.int32)
        slot_c = column(slot_r).astype(jnp.int32)
        match = slot_c == lax.broadcasted_iota(jnp.int32, (BLK, SLOTS), 1)
        number = lax.broadcasted_iota(jnp.int32, (BLK, SLOTS), 0).astype(F32)
        filled = jnp.sum(jnp.where(match, 1.0, 0.0), axis=0, keepdims=True)
        source = jnp.sum(jnp.where(match, number, 0.0), axis=0, keepdims=True)
        line = jnp.sum(jnp.where(match, line_c, 0.0), axis=0, keepdims=True)
        return slot_r, filled, source.astype(jnp.int32), line.astype(jnp.int32)

    out[...] = jnp.zeros((8, SLOTS), jnp.int32)
    _, filled, source, line = one(ed[...], el[...])
    out[0:1, :] = jnp.where(filled > 0.5, source, BLK)
    out[1:2, :] = line
    slot, _, source, line = one(dd[...], dl[...])
    out[2:3, :] = source
    out[3:4, :] = line
    out[4:5, 0:BLK] = slot


def encode_kernel(route, feat, pos, out, terms):
    step = pl.program_id(0)

    @pl.when(step == 0)
    def _():
        terms[BLK] = jnp.zeros((C, NZ), F32)

    @pl.when(step < 8)
    def _():
        grid_cells = lax.broadcasted_iota(jnp.int32, (NZ, PB), 0).astype(F32)
        for b in range(16):
            a, o, t = pos[0, b : b + 1, :], pos[1, b : b + 1, :], pos[2, b : b + 1, :]
            radial = jnp.exp((a * a + o * o) * (-1.0 / (2.0 * radius_scale**2)))
            offset = grid_cells - (t + 1.0) * (0.5 * (NZ - 1))
            rows = jnp.exp(offset * offset * (-1.0 / (2.0 * spread_cells**2)))
            fh, fl = split(feat[b] * radial)
            kh, kl = split(rows)
            both = nt(jnp.concatenate([fh, fl], axis=0), kh)
            terms[step * 16 + b] = both[:C] + (both[C:] + nt(fh, kl))

    @pl.when(step >= 8)
    def _():
        base = (step - 8) * 48

        def put(i, carry):
            out[i] = terms[route[0, base + i]]
            return carry

        lax.fori_loop(0, 48, put, 0, unroll=8)


def queries_kernel(route, pos, out):
    lane = lax.broadcasted_iota(jnp.int32, (1, 128), 1)

    def peer(d, carry):
        tags = jnp.zeros((1, 128), F32)
        for r in range(CAP):
            s = d * CAP + r
            for part in range(3):
                out[d, 3 * r + part : 3 * r + part + 1, :] = pos[part, pl.ds(route[2, s], 1), :]
            tags = jnp.where(lane == r, route[3, s].astype(F32), tags)
            tags = jnp.where(lane == CAP + r, route[1, s].astype(F32), tags)
        out[d, 18:19, :] = tags
        out[d, 19:24, :] = jnp.zeros((5, 128), F32)
        return carry

    lax.fori_loop(0, SLABS, peer, 0)


def profile_kernel(pos, out):
    step = pl.program_id(0)
    grid_cells = lax.broadcasted_iota(jnp.int32, (NZ, PB), 0).astype(F32)

    def one(d, carry):
        for r in range(CAP):
            a = pos[d, 3 * r : 3 * r + 1, :]
            o = pos[d, 3 * r + 1 : 3 * r + 2, :]
            t = pos[d, 3 * r + 2 : 3 * r + 3, :]
            radial = jnp.exp((a * a + o * o) * (-1.0 / (2.0 * radius_scale**2)))
            offset = grid_cells - (t + 1.0) * (0.5 * (NZ - 1))
            rows = jnp.exp(offset * offset * (-1.0 / (2.0 * spread_cells**2))) * radial
            kh, kl = split(rows)
            out[d * CAP + r, :, 0:PB] = kh
            out[d * CAP + r, :, PB : 2 * PB] = kl
        return carry

    lax.fori_loop(0, 4, one, 0)


def forward_kernel(tags, got, dy, fz, latent, message, scratch):
    step = pl.program_id(0)

    @pl.when(step == 0)
    def _():
        latent[...] = jnp.zeros_like(latent)

    for q in range(8):
        for r in range(CAP):
            line = tags[step * 8 + q, CAP + r]
            start = pl.multiple_of(line * C, C)
            latent[pl.ds(start, C), :] += got[q * CAP + r]

    @pl.when(step == 7)
    def _():
        def quad(i, carry):
            plane = i // (C // 4)
            channel = (i % (C // 4)) * 4
            start = plane * NY * C + channel
            data = jnp.concatenate(
                [latent[pl.ds(start + n, NY, stride=C), :] for n in range(4)], axis=1
            )
            y = mm(dy[...], right3(data))
            x = jnp.concatenate(
                [
                    jnp.concatenate(
                        [y[:MY, n * NZ : n * NZ + NZ], y[MY:, n * NZ : n * NZ + NZ]], axis=1
                    )
                    for n in range(4)
                ],
                axis=0,
            )
            at = pl.multiple_of((plane * C + channel) * MY, MY)
            scratch[pl.ds(at, 4 * MY), :] = mm(left3(x), fz[...])
            return carry

        lax.fori_loop(0, PLANES * C // 4, quad, 0, unroll=2)

        def flip(j, carry):
            turned = jnp.transpose(scratch[pl.ds(j, PLANES * C, stride=MY), :])
            message[j, :, 0:64] = turned[:MROWS]
            message[j, :, 64:128] = turned[64 : 64 + MROWS]
            return carry

        lax.fori_loop(0, MY, flip, 0, unroll=4)


def skip_kernel(kron, bias, latent, out):
    for n in range(4):
        rows = slice(n * 256, n * 256 + 256)
        out[rows, :] = mm(kron[...], right3(latent[rows, :])) + bias[...]


def planes_of(t, first_plane):
    u = jnp.where(first_plane, t[0:64], t[64:128])
    w = jnp.where(first_plane, t[128:192], t[192:256])
    return u, pltpu.roll(w, 64, 1)


def mix_rows(spec, weight, fx, spread, gather, ix, out, pitch, row, kz, count):
    lane = lax.broadcasted_iota(jnp.int32, (64, 128), 1)
    first_plane = (lane & 32) == 0
    real_part = lane < 64
    data = jnp.concatenate(
        [spec[pl.ds(row + n, SLABS, stride=pitch), :] for n in range(count)], axis=1
    )
    t = mm(fx[...], right3(data))
    rows = []
    for n in range(count):
        u, w = planes_of(t[:, n * 128 : n * 128 + 128], first_plane)
        rows.append(u + jnp.where(real_part, w, -w))
    sh, sl = split(jnp.concatenate(rows, axis=0))
    wide = mm(jnp.concatenate([sh, sl], axis=1), spread[...])
    rows = []
    for n in range(count):
        acc_re = jnp.zeros((64, 128), F32)
        acc_im = jnp.zeros((64, 128), F32)
        part = slice(n * 64, n * 64 + 64)
        for piece in range(8):
            re = slice(piece * 128, piece * 128 + 128)
            im = slice(C * C + piece * 128, C * C + piece * 128 + 128)
            w_re = weight[kz + n, :, re].astype(F32)
            w_im = weight[kz + n, :, im].astype(F32)
            acc_re += wide[part, re] * w_re - wide[part, im] * w_im
            acc_im += wide[part, re] * w_im + wide[part, im] * w_re
        rows.append(jnp.concatenate([acc_re, acc_im], axis=1))
    ah, al = split(jnp.concatenate(rows, axis=0))
    o = mm(jnp.concatenate([ah, al], axis=1), gather[...])
    data = jnp.concatenate([o[n * 64 : n * 64 + 64] for n in range(count)], axis=1)
    t = mm(ix[...], right3(data))
    for n in range(count):
        u, w = planes_of(t[:, n * 128 : n * 128 + 128], first_plane)
        out[pl.ds(row + n, SLABS, stride=pitch), :] = u + jnp.where(real_part, -w, w)


GROUPS = ((0, 16, 16), (16, 16, 16), (32, 1, 8))


def mix_kernel(
    message, weight_far, fx, spread, gather, ix, out,
    spec_0, spec_1, spec_2, ready_0, ready_1, ready_2, weight,
    send_a, recv_a, send_b, recv_b, weight_sem,
):
    specs, readies = (spec_0, spec_1, spec_2), (ready_0, ready_1, ready_2)
    me = lax.axis_index("slab")
    barrier = pltpu.get_barrier_semaphore()
    mesh_id = pl.DeviceIdType.MESH

    def greet(k, carry):
        peer = lax.rem(me + k, SLABS)
        pl.semaphore_signal(barrier, inc=1, device_id={"slab": peer}, device_id_type=mesh_id)
        return carry

    lax.fori_loop(1, SLABS, greet, 0)
    fetch = pltpu.make_async_copy(weight_far, weight, weight_sem)
    fetch.start()
    for group, (first, count, pitch) in enumerate(GROUPS):
        near = pl.multiple_of(me * pitch, 8)
        far = pl.multiple_of(me * MROWS + first, 8)
        specs[group][pl.ds(near, pitch), :] = message[pl.ds(far, pitch), :]
    pl.semaphore_wait(barrier, SLABS - 1)

    def scatter(source, target, send, recv, group, source_pitch, target_pitch, count):
        def go(k, carry):
            peer = lax.rem(me + lax.rem(k * 27, SLABS), SLABS)
            theirs = pl.multiple_of(peer * source_pitch[0] + source_pitch[1], 8)
            mine = pl.multiple_of(me * target_pitch[0] + target_pitch[1], 8)
            pltpu.make_async_remote_copy(
                src_ref=source.at[pl.ds(theirs, count)],
                dst_ref=target.at[pl.ds(mine, count)],
                send_sem=send.at[group],
                recv_sem=recv.at[group],
                device_id={"slab": peer},
                device_id_type=mesh_id,
            ).start()
            return carry

        lax.fori_loop(1, SLABS, go, 0)

    def settle(ref, sem, group, count):
        part = ref.at[pl.ds(0, (SLABS - 1) * count)]
        pltpu.make_async_copy(part, part, sem.at[group]).wait()

    for group, (first, count, pitch) in enumerate(GROUPS):
        scatter(message, specs[group], send_a, recv_a, group, (MROWS, first), (pitch, 0), count)
    fetch.wait()
    for group, (first, count, pitch) in enumerate(GROUPS):
        spec, ready = specs[group], readies[group]
        settle(spec, recv_a, group, count)
        if count == 1:
            ready[...] = jnp.zeros_like(ready)
            mix_rows(spec, weight, fx, spread, gather, ix, ready, pitch, 0, first, 1)
        else:

            def four(i, carry):
                row = 4 * i
                mix_rows(spec, weight, fx, spread, gather, ix, ready, pitch, row, first + row, 4)
                return carry

            lax.fori_loop(0, count // 4, four, 0)
        scatter(ready, out, send_b, recv_b, group, (pitch, 0), (MROWS, first), count)
        near = pl.multiple_of(me * pitch, 8)
        far = pl.multiple_of(me * MROWS + first, 8)
        out[pl.ds(far, pitch), :] = ready[pl.ds(near, pitch), :]
    for group, (first, count, pitch) in enumerate(GROUPS):
        settle(message, send_a, group, count)
        settle(readies[group], send_b, group, count)
        settle(out, recv_b, group, count)


def decode_kernel(tags, inverse, base, profile, iy, iz, dw, ow, out, modes, hidden):
    step = pl.program_id(0)

    @pl.when(step == 0)
    def _():
        lane = lax.broadcasted_iota(jnp.int32, (NY, 128), 1)
        real_part = lane < 64

        def clear(n, carry):
            modes[pl.ds(pl.multiple_of(n * 64 + 32, 32), 32), :] = jnp.zeros((32, 128), F32)
            return carry

        lax.fori_loop(0, NY, clear, 0, unroll=8)

        def planes(i, carry):
            data = jnp.concatenate(
                [inverse[pl.ds(i * 3 + n, MY, stride=MROWS), :] for n in range(3)], axis=1
            )
            t = mm(iy[...], right3(data))
            for n in range(3):
                cols = slice(n * 128, n * 128 + 128)
                w = pltpu.roll(t[NY:, cols], 64, 1)
                modes[pl.ds(i * 3 + n, NY, stride=64), :] = t[:NY, cols] + jnp.where(
                    real_part, -w, w
                )
            return carry

        lax.fori_loop(0, MZ // 3, planes, 0)

        def columns(i, carry):
            rows = []
            for n in range(4):
                at = pl.multiple_of((i * 4 + n) * 128, 128)
                turned = jnp.transpose(modes[pl.ds(at, 128), :])
                rows.append(jnp.concatenate([turned[:64], turned[64:]], axis=1))
            s = mm(left3(jnp.concatenate(rows, axis=0)), iz[...])
            for n in range(4):
                for plane in range(PLANES):
                    for twin in range(2):
                        at = pl.multiple_of((plane * NY + 2 * (i * 4 + n) + twin) * C, C)
                        top = n * 64 + plane * C
                        value = s[top : top + C, twin * NZ : twin * NZ + NZ] + base[pl.ds(at, C), :]
                        hidden[pl.ds(at, C), :] = jax.nn.gelu(value)
            return carry

        lax.fori_loop(0, NY // 8, columns, 0)

    for pair in range(2):
        sides = []
        for half in range(2):
            near = []
            for i in range(6):
                q = (pair * 2 + half) * 6 + i
                line = tags[step * 4 + pair * 2 + half, i]
                hh, hl = split(hidden[pl.ds(pl.multiple_of(line * C, C), C), :])
                both = mm(jnp.concatenate([hh, hl], axis=0), profile[q])
                near.append(both[:C, :PB] + (both[C:, :PB] + both[:C, PB:]))
            sides.append(jnp.concatenate(near, axis=0))
        act = jax.nn.gelu(mm(dw[...], right3(jnp.concatenate(sides, axis=1))))
        result = mm(ow[...], right3(act))
        for half in range(2):
            d = pair * 2 + half
            out[d] = result[:, half * PB : half * PB + PB]


def local(
    enc_feat,
    enc_pos,
    enc_dest,
    enc_line,
    dec_pos,
    dec_dest,
    dec_line,
    mode_weight,
    skip_weight,
    skip_bias,
    dec_weight,
    out_weight,
):
    forward_y, inverse_y, forward_z, inverse_z, forward_x, inverse_x, spread, gather = tables()
    exchange = functools.partial(
        lax.all_to_all, axis_name="slab", split_axis=0, concat_axis=0, tiled=True
    )
    route = pl.pallas_call(
        routes_kernel, out_shape=jax.ShapeDtypeStruct((8, SLOTS), jnp.int32), name="routes"
    )(
        enc_dest.reshape(1, BLK),
        enc_line.reshape(1, BLK),
        dec_dest.reshape(1, BLK),
        dec_line.reshape(1, BLK),
    )
    queries = pl.pallas_call(
        queries_kernel,
        out_shape=jax.ShapeDtypeStruct((SLABS, QROWS, 128), F32),
        in_specs=[SMEM, whole((3, BLK, PB))],
        out_specs=whole((SLABS, QROWS, 128)),
        name="queries",
    )(route, jnp.transpose(dec_pos, (1, 0, 2)))
    packed = pl.pallas_call(
        encode_kernel,
        out_shape=jax.ShapeDtypeStruct((SLOTS, C, NZ), F32),
        grid=(16,),
        in_specs=[
            SMEM,
            pl.BlockSpec((16, C, PB), lambda i: (jnp.minimum(i, 7), 0, 0)),
            pl.BlockSpec((3, 16, PB), lambda i: (0, jnp.minimum(i, 7), 0)),
        ],
        out_specs=pl.BlockSpec((48, C, NZ), lambda i: (jnp.maximum(i - 8, 0), 0, 0)),
        scratch_shapes=[pltpu.VMEM((BLK + 1, C, NZ), F32)],
        compiler_params=params(),
        cost_estimate=cost(12),
        name="encode",
    )(route, enc_feat, jnp.transpose(enc_pos, (1, 0, 2)))
    got_queries = exchange(queries)
    got_terms = exchange(packed)
    tags = got_queries[:, 18, 0 : 2 * CAP].astype(jnp.int32)
    profile = pl.pallas_call(
        profile_kernel,
        out_shape=jax.ShapeDtypeStruct((SLOTS, NZ, 2 * PB), BF),
        grid=(16,),
        in_specs=[pl.BlockSpec((4, QROWS, PB), lambda i: (i, 0, 0))],
        out_specs=pl.BlockSpec((24, NZ, 2 * PB), lambda i: (i, 0, 0)),
        compiler_params=params(),
        cost_estimate=cost(25),
        name="profile",
    )(got_queries)
    tags, profile = lax.optimization_barrier((tags, profile))
    skip_wide = left_table(jnp.kron(jnp.eye(8, dtype=F32), skip_weight.T))
    skip_bias_wide = jnp.tile(skip_bias, 8)[:, None]
    dec_wide = left_table(jnp.kron(jnp.eye(CAP, dtype=F32), dec_weight.T))
    out_wide = left_table(jnp.kron(jnp.eye(CAP, dtype=F32), out_weight[None, :]))
    latent, message = pl.pallas_call(
        forward_kernel,
        out_shape=(
            jax.ShapeDtypeStruct((LINES * C, NZ), F32),
            jax.ShapeDtypeStruct((MY, MROWS, 128), F32),
        ),
        grid=(8,),
        in_specs=[
            SMEM,
            pl.BlockSpec((48, C, NZ), lambda i: (i, 0, 0)),
            whole((2 * MY, 3 * NY)),
            whole((6 * NZ, 128)),
        ],
        out_specs=(whole((LINES * C, NZ)), whole((MY, MROWS, 128))),
        scratch_shapes=[pltpu.VMEM((PLANES * C * MY, 128), F32)],
        compiler_params=params(),
        name="forward",
    )(tags, got_terms, forward_y, forward_z)
    base = pl.pallas_call(
        skip_kernel,
        out_shape=jax.ShapeDtypeStruct((LINES * C, NZ), F32),
        grid=(8,),
        in_specs=[
            whole((256, 768)),
            whole((256, 1)),
            pl.BlockSpec((1024, NZ), lambda i: (i, 0)),
        ],
        out_specs=pl.BlockSpec((1024, NZ), lambda i: (i, 0)),
        compiler_params=params(),
        cost_estimate=cost(12),
        name="skip",
    )(skip_wide, skip_bias_wide, latent)
    weight = jnp.transpose(mode_weight.reshape(MX, MZ, 2 * C * C), (1, 0, 2))
    vm = pl.BlockSpec(memory_space=pltpu.VMEM)
    inverse = pl.pallas_call(
        mix_kernel,
        out_shape=jax.ShapeDtypeStruct((SLABS * MROWS, 128), F32),
        in_specs=[vm, pl.BlockSpec(memory_space=pl.ANY), vm, vm, vm, vm],
        out_specs=vm,
        scratch_shapes=[
            *[pltpu.VMEM((SLABS * pitch, 128), F32) for _, _, pitch in GROUPS],
            *[pltpu.VMEM((SLABS * pitch, 128), F32) for _, _, pitch in GROUPS],
            pltpu.VMEM((MZ, MX, 2 * C * C), BF),
            pltpu.SemaphoreType.DMA((3,)),
            pltpu.SemaphoreType.DMA((3,)),
            pltpu.SemaphoreType.DMA((3,)),
            pltpu.SemaphoreType.DMA((3,)),
            pltpu.SemaphoreType.DMA,
        ],
        compiler_params=params(collective_id=0, has_side_effects=True),
        name="mix",
    )(message.reshape(SLABS * MROWS, 128), weight, forward_x, spread, gather, inverse_x)
    answers = pl.pallas_call(
        decode_kernel,
        out_shape=jax.ShapeDtypeStruct((SLABS, CAP, PB), F32),
        grid=(16,),
        in_specs=[
            SMEM,
            whole((MY * MROWS, 128)),
            whole((LINES * C, NZ)),
            pl.BlockSpec((24, NZ, 2 * PB), lambda i: (i, 0, 0)),
            whole((2 * NY, 192)),
            whole((768, 2 * NZ)),
            whole((CAP * C, 3 * CAP * C)),
            whole((CAP, 3 * CAP * C)),
        ],
        out_specs=pl.BlockSpec((4, CAP, PB), lambda i: (i, 0, 0)),
        scratch_shapes=[
            pltpu.VMEM((NY * 64, 128), F32),
            pltpu.VMEM((LINES * C, NZ), F32),
        ],
        compiler_params=params(),
        name="decode",
    )(
        tags,
        inverse,
        base,
        profile,
        inverse_y,
        inverse_z,
        dec_wide,
        out_wide,
    )
    returned = exchange(answers)
    slot = route[4, 0:BLK]
    return returned[slot // CAP, slot % CAP]


def solution(mesh):
    placed = (
        P(("geo", "slab"), None, None),
        P(("geo", "slab"), None, None),
        P(("geo", "slab"), None),
        P(("geo", "slab")),
        P(("geo", "slab"), None, None),
        P(("geo", "slab"), None),
        P(("geo", "slab")),
        P(None, "slab", None, None),
        P(),
        P(),
        P(),
        P(),
    )
    return jax.shard_map(
        local, mesh=mesh, in_specs=placed, out_specs=P(("geo", "slab"), None), check_vma=False
    )
```

```python
import functools
import math

import jax
import jax.numpy as jnp
import numpy as np
from jax import lax
from jax.experimental import pallas as pl
from jax.experimental.pallas import tpu as pltpu
from jax.sharding import PartitionSpec as P

C = 32
NX = 128
NY = 128
NZ = 128
MX = 64
MY = 64
MZ = 33
PB = 128
BLK = 128
SLABS = 64
PLANES = NX // SLABS
CAP = 6
SLOTS = SLABS * CAP
LINES = PLANES * NY
MROWS = 40
QROWS = 24
VMEM_LIMIT = 60 * 1024 * 1024

radius_scale = 0.7
spread_cells = 1.5
BF = jnp.bfloat16
F32 = jnp.float32


def split_np(table):
    table = np.asarray(table, np.float32)
    high = table.astype(jnp.bfloat16)
    low = (table - high.astype(np.float32)).astype(jnp.bfloat16)
    return high, low


def left_np(table):
    high, low = split_np(table)
    return np.concatenate([high, low, high], axis=1)


def right_np(table):
    high, low = split_np(table)
    return np.concatenate([high, high, low], axis=0)


def split(values):
    high = values.astype(BF)
    low = (values - high.astype(F32)).astype(BF)
    return high, low


def left_table(values):
    high = lax.reduce_precision(values, 8, 7)
    low = (values - high).astype(BF)
    high = high.astype(BF)
    return jnp.concatenate([high, low, high], axis=1)


def left3(values):
    high, low = split(values)
    return jnp.concatenate([high, low, high], axis=1)


def right3(values):
    high, low = split(values)
    return jnp.concatenate([high, high, low], axis=0)


def mm(left, right):
    return jnp.dot(left, right, preferred_element_type=F32)


def nt(left, right):
    return lax.dot_general(left, right, (((1,), (1,)), ((), ())), preferred_element_type=F32)


def kept(length, count):
    counter = np.arange(count)
    return np.where(counter < count // 2, counter, counter + length - count)


def tables():
    cells = np.arange(NY)
    ky = kept(NY, MY)
    angle = 2.0 * math.pi * ((ky[:, None] * cells[None, :]) % NY) / NY
    cos_y, sin_y = np.cos(angle), np.sin(angle)
    forward_y = np.concatenate([cos_y, -sin_y], axis=0)
    inverse_y = np.concatenate([cos_y.T, sin_y.T], axis=0) / NY
    z_angle = 2.0 * math.pi * ((np.arange(NZ)[:, None] * np.arange(MZ)[None, :]) % NZ) / NZ
    cos_z, sin_z = np.cos(z_angle), np.sin(z_angle)
    forward_z = np.zeros((2 * NZ, 128))
    forward_z[:NZ, :MZ] = cos_z
    forward_z[:NZ, 64 : 64 + MZ] = -sin_z
    forward_z[NZ:, :MZ] = sin_z
    forward_z[NZ:, 64 : 64 + MZ] = cos_z
    weight = np.where(np.arange(MZ) == 0, 1.0, 2.0) / NZ
    inverse_z = np.zeros((2, 2, 64, 2, NZ))
    for twin in range(2):
        inverse_z[0, twin, :MZ, twin, :] = (cos_z * weight[None, :]).T
        inverse_z[1, twin, :MZ, twin, :] = -(sin_z * weight[None, :]).T
    inverse_z = inverse_z.reshape(256, 256)
    kx = kept(NX, MX)
    owner = np.arange(SLABS)
    forward_x, inverse_x = [], []
    for part in (np.cos, np.sin):
        for plane in range(PLANES):
            turns = (kx[:, None] * (PLANES * owner + plane)[None, :]) % NX
            table = part(2.0 * math.pi * turns / NX)
            forward_x.append(table)
            inverse_x.append(table.T / NX)
    forward_x = np.concatenate(forward_x, axis=0)
    inverse_x = np.concatenate(inverse_x, axis=0)
    spread = np.zeros((2, PLANES, C, 2, C, C))
    for channel in range(C):
        for part in range(2):
            spread[part, :, channel, part, channel, :] = 1.0
    spread = spread.reshape(128, 2 * C * C)
    gather = np.zeros((2, 4, C, 2, PLANES, C))
    for channel in range(C):
        for part in range(2):
            gather[part, :, channel, part, :, channel] = 1.0
    gather = gather.reshape(256, 128)
    return (
        left_np(forward_y),
        left_np(inverse_y),
        right_np(forward_z),
        right_np(inverse_z),
        left_np(forward_x),
        left_np(inverse_x),
        np.asarray(np.concatenate([spread, spread], axis=0), jnp.bfloat16),
        np.asarray(np.concatenate([gather, gather], axis=0), jnp.bfloat16),
    )


def params(**extra):
    return pltpu.CompilerParams(vmem_limit_bytes=VMEM_LIMIT, **extra)


def cost(microseconds):
    return pl.CostEstimate(
        flops=0, transcendentals=0, bytes_accessed=int(microseconds * 2_000_000)
    )


def whole(shape):
    return pl.BlockSpec(shape, lambda *_: (0,) * len(shape))


SMEM = pl.BlockSpec(memory_space=pltpu.SMEM)


def routes_kernel(ed, el, dd, dl, out):
    rows = lax.broadcasted_iota(jnp.int32, (BLK, BLK), 0)
    cols = lax.broadcasted_iota(jnp.int32, (BLK, BLK), 1)

    def column(row):
        spread_row = jnp.broadcast_to(row.astype(F32), (BLK, BLK))
        return jnp.sum(jnp.where(rows == cols, spread_row, 0.0), axis=1, keepdims=True)

    def one(dest_r, line_r):
        dest_c = column(dest_r).astype(jnp.int32)
        line_c = column(line_r)
        same = dest_c == dest_r
        before_r = jnp.sum(jnp.where(same & (rows < cols), 1.0, 0.0), axis=0, keepdims=True)
        slot_r = dest_r * CAP + before_r.astype(jnp.int32)
        slot_c = column(slot_r).astype(jnp.int32)
        match = slot_c == lax.broadcasted_iota(jnp.int32, (BLK, SLOTS), 1)
        number = lax.broadcasted_iota(jnp.int32, (BLK, SLOTS), 0).astype(F32)
        filled = jnp.sum(jnp.where(match, 1.0, 0.0), axis=0, keepdims=True)
        source = jnp.sum(jnp.where(match, number, 0.0), axis=0, keepdims=True)
        line = jnp.sum(jnp.where(match, line_c, 0.0), axis=0, keepdims=True)
        return dest_r * 8 + before_r.astype(jnp.int32), filled, source.astype(jnp.int32), line.astype(jnp.int32)

    out[...] = jnp.zeros((8, SLOTS), jnp.int32)
    _, filled, source, line = one(ed[...], el[...])
    out[0:1, :] = jnp.where(filled > 0.5, source, BLK)
    out[1:2, :] = line
    slot, _, source, line = one(dd[...], dl[...])
    out[2:3, :] = source
    out[3:4, :] = line
    out[4:5, 0:BLK] = slot


def encode_kernel(route, feat, pos, out, terms):
    step = pl.program_id(0)

    @pl.when(step == 0)
    def _():
        terms[BLK] = jnp.zeros((C, NZ), F32)

    @pl.when(step < 8)
    def _():
        grid_cells = lax.broadcasted_iota(jnp.int32, (NZ, PB), 0).astype(F32)
        for b in range(16):
            a, o, t = pos[0, b : b + 1, :], pos[1, b : b + 1, :], pos[2, b : b + 1, :]
            radial = jnp.exp((a * a + o * o) * (-1.0 / (2.0 * radius_scale**2)))
            offset = grid_cells - (t + 1.0) * (0.5 * (NZ - 1))
            rows = jnp.exp(offset * offset * (-1.0 / (2.0 * spread_cells**2)))
            fh, fl = split(feat[b] * radial)
            kh, kl = split(rows)
            both = nt(jnp.concatenate([fh, fl], axis=0), kh)
            terms[step * 16 + b] = both[:C] + (both[C:] + nt(fh, kl))

    @pl.when(step >= 8)
    def _():
        base = (step - 8) * 48

        def put(i, carry):
            out[i] = terms[route[0, base + i]]
            return carry

        lax.fori_loop(0, 48, put, 0, unroll=8)


def queries_kernel(route, pos, out):
    lane = lax.broadcasted_iota(jnp.int32, (1, 128), 1)

    def peer(d, carry):
        tags = jnp.zeros((1, 128), F32)
        for r in range(CAP):
            s = d * CAP + r
            for part in range(3):
                out[d, 3 * r + part : 3 * r + part + 1, :] = pos[part, pl.ds(route[2, s], 1), :]
            tags = jnp.where(lane == r, route[3, s].astype(F32), tags)
            tags = jnp.where(lane == CAP + r, route[1, s].astype(F32), tags)
        out[d, 18:19, :] = tags
        out[d, 19:24, :] = jnp.zeros((5, 128), F32)
        return carry

    lax.fori_loop(0, SLABS, peer, 0)


def profile_kernel(pos, out):
    step = pl.program_id(0)
    grid_cells = lax.broadcasted_iota(jnp.int32, (NZ, PB), 0).astype(F32)

    def one(d, carry):
        for r in range(CAP):
            a = pos[d, 3 * r : 3 * r + 1, :]
            o = pos[d, 3 * r + 1 : 3 * r + 2, :]
            t = pos[d, 3 * r + 2 : 3 * r + 3, :]
            radial = jnp.exp((a * a + o * o) * (-1.0 / (2.0 * radius_scale**2)))
            offset = grid_cells - (t + 1.0) * (0.5 * (NZ - 1))
            rows = jnp.exp(offset * offset * (-1.0 / (2.0 * spread_cells**2))) * radial
            kh, kl = split(rows)
            out[d * CAP + r, :, 0:PB] = kh
            out[d * CAP + r, :, PB : 2 * PB] = kl
        return carry

    lax.fori_loop(0, 4, one, 0)


def forward_kernel(tags, got, dy, fz, latent, message, scratch):
    step = pl.program_id(0)

    @pl.when(step == 0)
    def _():
        latent[...] = jnp.zeros_like(latent)

    for q in range(8):
        for r in range(CAP):
            line = tags[step * 8 + q, CAP + r]
            start = pl.multiple_of(line * C, C)
            latent[pl.ds(start, C), :] += got[q * CAP + r]

    @pl.when(step == 7)
    def _():
        def quad(i, carry):
            plane = i // (C // 4)
            channel = (i % (C // 4)) * 4
            start = plane * NY * C + channel
            data = jnp.concatenate(
                [latent[pl.ds(start + n, NY, stride=C), :] for n in range(4)], axis=1
            )
            y = mm(dy[...], right3(data))
            x = jnp.concatenate(
                [
                    jnp.concatenate(
                        [y[:MY, n * NZ : n * NZ + NZ], y[MY:, n * NZ : n * NZ + NZ]], axis=1
                    )
                    for n in range(4)
                ],
                axis=0,
            )
            at = pl.multiple_of((plane * C + channel) * MY, MY)
            scratch[pl.ds(at, 4 * MY), :] = mm(left3(x), fz[...])
            return carry

        lax.fori_loop(0, PLANES * C // 4, quad, 0, unroll=2)

        def flip(j, carry):
            turned = jnp.transpose(scratch[pl.ds(j, PLANES * C, stride=MY), :])
            message[j, :, 0:64] = turned[:MROWS]
            message[j, :, 64:128] = turned[64 : 64 + MROWS]
            return carry

        lax.fori_loop(0, MY, flip, 0, unroll=4)


def planes_of(t, first_plane):
    u = jnp.where(first_plane, t[0:64], t[64:128])
    w = jnp.where(first_plane, t[128:192], t[192:256])
    return u, pltpu.roll(w, 64, 1)


def mix_rows(spec, weight, fx, spread, gather, ix, out, pitch, row, kz, count):
    lane = lax.broadcasted_iota(jnp.int32, (64, 128), 1)
    first_plane = (lane & 32) == 0
    real_part = lane < 64
    data = jnp.concatenate(
        [spec[pl.ds(row + n, SLABS, stride=pitch), :] for n in range(count)], axis=1
    )
    t = mm(fx[...], right3(data))
    rows = []
    for n in range(count):
        u, w = planes_of(t[:, n * 128 : n * 128 + 128], first_plane)
        rows.append(u + jnp.where(real_part, w, -w))
    sh, sl = split(jnp.concatenate(rows, axis=0))
    wide = mm(jnp.concatenate([sh, sl], axis=1), spread[...])
    rows = []
    for n in range(count):
        acc_re = jnp.zeros((64, 128), F32)
        acc_im = jnp.zeros((64, 128), F32)
        part = slice(n * 64, n * 64 + 64)
        for piece in range(8):
            re = slice(piece * 128, piece * 128 + 128)
            im = slice(C * C + piece * 128, C * C + piece * 128 + 128)
            w_re = weight[kz + n, :, re].astype(F32)
            w_im = weight[kz + n, :, im].astype(F32)
            acc_re += wide[part, re] * w_re - wide[part, im] * w_im
            acc_im += wide[part, re] * w_im + wide[part, im] * w_re
        rows.append(jnp.concatenate([acc_re, acc_im], axis=1))
    ah, al = split(jnp.concatenate(rows, axis=0))
    o = mm(jnp.concatenate([ah, al], axis=1), gather[...])
    data = jnp.concatenate([o[n * 64 : n * 64 + 64] for n in range(count)], axis=1)
    t = mm(ix[...], right3(data))
    for n in range(count):
        u, w = planes_of(t[:, n * 128 : n * 128 + 128], first_plane)
        out[pl.ds(row + n, SLABS, stride=pitch), :] = u + jnp.where(real_part, -w, w)


GROUPS = ((0, 16, 16), (16, 16, 16), (32, 1, 8))


def mix_kernel(
    message, weight_far, latent, fx, spread, gather, ix, kron, bias, out, base,
    spec_0, spec_1, spec_2, ready_0, ready_1, ready_2, weight, field,
    send_a, recv_a, send_b, recv_b, weight_sem, field_sem,
):
    specs, readies = (spec_0, spec_1, spec_2), (ready_0, ready_1, ready_2)
    me = lax.axis_index("slab")
    barrier = pltpu.get_barrier_semaphore()
    mesh_id = pl.DeviceIdType.MESH

    def greet(k, carry):
        peer = lax.rem(me + k, SLABS)
        pl.semaphore_signal(barrier, inc=1, device_id={"slab": peer}, device_id_type=mesh_id)
        return carry

    lax.fori_loop(1, SLABS, greet, 0)
    fetch = pltpu.make_async_copy(weight_far, weight, weight_sem)
    fetch.start()
    bring = pltpu.make_async_copy(latent, field, field_sem.at[0])
    bring.start()
    for group, (first, count, pitch) in enumerate(GROUPS):
        near = pl.multiple_of(me * pitch, 8)
        far = pl.multiple_of(me * MROWS + first, 8)
        specs[group][pl.ds(near, pitch), :] = message[pl.ds(far, pitch), :]
    pl.semaphore_wait(barrier, SLABS - 1)

    def scatter(source, target, send, recv, group, source_pitch, target_pitch, count):
        def go(k, carry):
            peer = lax.rem(me + lax.rem(k * 27, SLABS), SLABS)
            theirs = pl.multiple_of(peer * source_pitch[0] + source_pitch[1], 8)
            mine = pl.multiple_of(me * target_pitch[0] + target_pitch[1], 8)
            pltpu.make_async_remote_copy(
                src_ref=source.at[pl.ds(theirs, count)],
                dst_ref=target.at[pl.ds(mine, count)],
                send_sem=send.at[group],
                recv_sem=recv.at[group],
                device_id={"slab": peer},
                device_id_type=mesh_id,
            ).start()
            return carry

        lax.fori_loop(1, SLABS, go, 0)

    def settle(ref, sem, group, count):
        part = ref.at[pl.ds(0, (SLABS - 1) * count)]
        pltpu.make_async_copy(part, part, sem.at[group]).wait()

    for group, (first, count, pitch) in enumerate(GROUPS):
        scatter(message, specs[group], send_a, recv_a, group, (MROWS, first), (pitch, 0), count)
    bring.wait()

    def skip(n, carry):
        rows = pl.ds(pl.multiple_of(n * 256, 256), 256)
        field[rows, :] = mm(kron[...], right3(field[rows, :])) + bias[...]
        return carry

    lax.fori_loop(0, LINES * C // 256, skip, 0)
    leave = pltpu.make_async_copy(field, base, field_sem.at[1])
    leave.start()
    fetch.wait()
    for group, (first, count, pitch) in enumerate(GROUPS):
        spec, ready = specs[group], readies[group]
        settle(spec, recv_a, group, count)
        if count == 1:
            ready[...] = jnp.zeros_like(ready)
            mix_rows(spec, weight, fx, spread, gather, ix, ready, pitch, 0, first, 1)
        else:

            def four(i, carry):
                row = 4 * i
                mix_rows(spec, weight, fx, spread, gather, ix, ready, pitch, row, first + row, 4)
                return carry

            lax.fori_loop(0, count // 4, four, 0)
        scatter(ready, out, send_b, recv_b, group, (pitch, 0), (MROWS, first), count)
        near = pl.multiple_of(me * pitch, 8)
        far = pl.multiple_of(me * MROWS + first, 8)
        out[pl.ds(far, pitch), :] = ready[pl.ds(near, pitch), :]
    for group, (first, count, pitch) in enumerate(GROUPS):
        settle(message, send_a, group, count)
        settle(readies[group], send_b, group, count)
        settle(out, recv_b, group, count)
    leave.wait()


def decode_kernel(tags, inverse, base, profile, iy, iz, dw, ow, out, modes, hidden):
    step = pl.program_id(0)

    @pl.when(step == 0)
    def _():
        lane = lax.broadcasted_iota(jnp.int32, (NY, 128), 1)
        real_part = lane < 64

        def clear(n, carry):
            modes[pl.ds(pl.multiple_of(n * 64 + 32, 32), 32), :] = jnp.zeros((32, 128), F32)
            return carry

        lax.fori_loop(0, NY, clear, 0, unroll=8)

        def planes(i, carry):
            data = jnp.concatenate(
                [inverse[pl.ds(i * 3 + n, MY, stride=MROWS), :] for n in range(3)], axis=1
            )
            t = mm(iy[...], right3(data))
            for n in range(3):
                cols = slice(n * 128, n * 128 + 128)
                w = pltpu.roll(t[NY:, cols], 64, 1)
                modes[pl.ds(i * 3 + n, NY, stride=64), :] = t[:NY, cols] + jnp.where(
                    real_part, -w, w
                )
            return carry

        lax.fori_loop(0, MZ // 3, planes, 0)

        def columns(i, carry):
            rows = []
            for n in range(4):
                at = pl.multiple_of((i * 4 + n) * 128, 128)
                turned = jnp.transpose(modes[pl.ds(at, 128), :])
                rows.append(jnp.concatenate([turned[:64], turned[64:]], axis=1))
            s = mm(left3(jnp.concatenate(rows, axis=0)), iz[...])
            for n in range(4):
                for plane in range(PLANES):
                    for twin in range(2):
                        at = pl.multiple_of((plane * NY + 2 * (i * 4 + n) + twin) * C, C)
                        top = n * 64 + plane * C
                        value = s[top : top + C, twin * NZ : twin * NZ + NZ] + base[pl.ds(at, C), :]
                        hidden[pl.ds(at, C), :] = jax.nn.gelu(value)
            return carry

        lax.fori_loop(0, NY // 8, columns, 0)

    for pair in range(2):
        sides = []
        for half in range(2):
            near = []
            for i in range(6):
                q = (pair * 2 + half) * 6 + i
                line = tags[step * 4 + pair * 2 + half, i]
                hh, hl = split(hidden[pl.ds(pl.multiple_of(line * C, C), C), :])
                both = mm(jnp.concatenate([hh, hl], axis=0), profile[q])
                near.append(both[:C, :PB] + (both[C:, :PB] + both[:C, PB:]))
            sides.append(jnp.concatenate(near, axis=0))
        act = jax.nn.gelu(mm(dw[...], right3(jnp.concatenate(sides, axis=1))))
        result = mm(ow[...], right3(act))
        for half in range(2):
            d = pair * 2 + half
            out[d * 8 : d * 8 + CAP, :] = result[:, half * PB : half * PB + PB]


def reply_kernel(answers, out, send_sem, recv_sem):
    me = lax.axis_index("slab")
    barrier = pltpu.get_barrier_semaphore()
    mesh_id = pl.DeviceIdType.MESH

    def greet(k, carry):
        peer = lax.rem(me + k, SLABS)
        pl.semaphore_signal(barrier, inc=1, device_id={"slab": peer}, device_id_type=mesh_id)
        return carry

    lax.fori_loop(1, SLABS, greet, 0)
    here = pl.multiple_of(me * 8, 8)
    out[pl.ds(here, 8), :] = answers[pl.ds(here, 8), :]
    pl.semaphore_wait(barrier, SLABS - 1)

    def go(k, carry):
        peer = lax.rem(me + lax.rem(k * 27, SLABS), SLABS)
        there = pl.multiple_of(peer * 8, 8)
        pltpu.make_async_remote_copy(
            src_ref=answers.at[pl.ds(there, CAP)],
            dst_ref=out.at[pl.ds(here, CAP)],
            send_sem=send_sem,
            recv_sem=recv_sem,
            device_id={"slab": peer},
            device_id_type=mesh_id,
        ).start()
        return carry

    lax.fori_loop(1, SLABS, go, 0)
    everything = pl.ds(0, (SLABS - 1) * CAP)
    came, sent = out.at[everything], answers.at[everything]
    pltpu.make_async_copy(came, came, recv_sem).wait()
    pltpu.make_async_copy(sent, sent, send_sem).wait()


def local(
    enc_feat,
    enc_pos,
    enc_dest,
    enc_line,
    dec_pos,
    dec_dest,
    dec_line,
    mode_weight,
    skip_weight,
    skip_bias,
    dec_weight,
    out_weight,
):
    forward_y, inverse_y, forward_z, inverse_z, forward_x, inverse_x, spread, gather = tables()
    exchange = functools.partial(
        lax.all_to_all, axis_name="slab", split_axis=0, concat_axis=0, tiled=True
    )
    route = pl.pallas_call(
        routes_kernel, out_shape=jax.ShapeDtypeStruct((8, SLOTS), jnp.int32), name="routes"
    )(
        enc_dest.reshape(1, BLK),
        enc_line.reshape(1, BLK),
        dec_dest.reshape(1, BLK),
        dec_line.reshape(1, BLK),
    )
    queries = pl.pallas_call(
        queries_kernel,
        out_shape=jax.ShapeDtypeStruct((SLABS, QROWS, 128), F32),
        in_specs=[SMEM, whole((3, BLK, PB))],
        out_specs=whole((SLABS, QROWS, 128)),
        name="queries",
    )(route, jnp.transpose(dec_pos, (1, 0, 2)))
    packed = pl.pallas_call(
        encode_kernel,
        out_shape=jax.ShapeDtypeStruct((SLOTS, C, NZ), F32),
        grid=(16,),
        in_specs=[
            SMEM,
            pl.BlockSpec((16, C, PB), lambda i: (jnp.minimum(i, 7), 0, 0)),
            pl.BlockSpec((3, 16, PB), lambda i: (0, jnp.minimum(i, 7), 0)),
        ],
        out_specs=pl.BlockSpec((48, C, NZ), lambda i: (jnp.maximum(i - 8, 0), 0, 0)),
        scratch_shapes=[pltpu.VMEM((BLK + 1, C, NZ), F32)],
        compiler_params=params(),
        cost_estimate=cost(12),
        name="encode",
    )(route, enc_feat, jnp.transpose(enc_pos, (1, 0, 2)))
    got_queries = exchange(queries)
    got_terms = exchange(packed)
    tags = got_queries[:, 18, 0 : 2 * CAP].astype(jnp.int32)
    profile = pl.pallas_call(
        profile_kernel,
        out_shape=jax.ShapeDtypeStruct((SLOTS, NZ, 2 * PB), BF),
        grid=(16,),
        in_specs=[pl.BlockSpec((4, QROWS, PB), lambda i: (i, 0, 0))],
        out_specs=pl.BlockSpec((24, NZ, 2 * PB), lambda i: (i, 0, 0)),
        compiler_params=params(),
        cost_estimate=cost(25),
        name="profile",
    )(got_queries)
    tags, profile = lax.optimization_barrier((tags, profile))
    skip_wide = left_table(jnp.kron(jnp.eye(8, dtype=F32), skip_weight.T))
    skip_bias_wide = jnp.tile(skip_bias, 8)[:, None]
    dec_wide = left_table(jnp.kron(jnp.eye(CAP, dtype=F32), dec_weight.T))
    out_wide = left_table(jnp.kron(jnp.eye(CAP, dtype=F32), out_weight[None, :]))
    latent, message = pl.pallas_call(
        forward_kernel,
        out_shape=(
            jax.ShapeDtypeStruct((LINES * C, NZ), F32),
            jax.ShapeDtypeStruct((MY, MROWS, 128), F32),
        ),
        grid=(8,),
        in_specs=[
            SMEM,
            pl.BlockSpec((48, C, NZ), lambda i: (i, 0, 0)),
            whole((2 * MY, 3 * NY)),
            whole((6 * NZ, 128)),
        ],
        out_specs=(whole((LINES * C, NZ)), whole((MY, MROWS, 128))),
        scratch_shapes=[pltpu.VMEM((PLANES * C * MY, 128), F32)],
        compiler_params=params(),
        name="forward",
    )(tags, got_terms, forward_y, forward_z)
    weight = jnp.transpose(mode_weight.reshape(MX, MZ, 2 * C * C), (1, 0, 2))
    vm = pl.BlockSpec(memory_space=pltpu.VMEM)
    far = pl.BlockSpec(memory_space=pl.ANY)
    inverse, base = pl.pallas_call(
        mix_kernel,
        out_shape=(
            jax.ShapeDtypeStruct((SLABS * MROWS, 128), F32),
            jax.ShapeDtypeStruct((LINES * C, NZ), F32),
        ),
        in_specs=[vm, far, far, vm, vm, vm, vm, vm, vm],
        out_specs=(vm, far),
        scratch_shapes=[
            *[pltpu.VMEM((SLABS * pitch, 128), F32) for _, _, pitch in GROUPS],
            *[pltpu.VMEM((SLABS * pitch, 128), F32) for _, _, pitch in GROUPS],
            pltpu.VMEM((MZ, MX, 2 * C * C), BF),
            pltpu.VMEM((LINES * C, NZ), F32),
            pltpu.SemaphoreType.DMA((3,)),
            pltpu.SemaphoreType.DMA((3,)),
            pltpu.SemaphoreType.DMA((3,)),
            pltpu.SemaphoreType.DMA((3,)),
            pltpu.SemaphoreType.DMA,
            pltpu.SemaphoreType.DMA((2,)),
        ],
        compiler_params=params(collective_id=0, has_side_effects=True),
        name="mix",
    )(
        message.reshape(SLABS * MROWS, 128),
        weight,
        latent,
        forward_x,
        spread,
        gather,
        inverse_x,
        skip_wide,
        skip_bias_wide,
    )
    answers = pl.pallas_call(
        decode_kernel,
        out_shape=jax.ShapeDtypeStruct((SLABS * 8, PB), F32),
        grid=(16,),
        in_specs=[
            SMEM,
            whole((MY * MROWS, 128)),
            whole((LINES * C, NZ)),
            pl.BlockSpec((24, NZ, 2 * PB), lambda i: (i, 0, 0)),
            whole((2 * NY, 192)),
            whole((768, 2 * NZ)),
            whole((CAP * C, 3 * CAP * C)),
            whole((CAP, 3 * CAP * C)),
        ],
        out_specs=pl.BlockSpec((32, PB), lambda i: (i, 0)),
        scratch_shapes=[
            pltpu.VMEM((NY * 64, 128), F32),
            pltpu.VMEM((LINES * C, NZ), F32),
        ],
        compiler_params=params(),
        name="decode",
    )(
        tags,
        inverse,
        base,
        profile,
        inverse_y,
        inverse_z,
        dec_wide,
        out_wide,
    )
    returned = pl.pallas_call(
        reply_kernel,
        out_shape=jax.ShapeDtypeStruct((SLABS * 8, PB), F32),
        in_specs=[vm],
        out_specs=vm,
        scratch_shapes=[pltpu.SemaphoreType.DMA, pltpu.SemaphoreType.DMA],
        compiler_params=params(collective_id=1, has_side_effects=True),
        name="reply",
    )(answers)
    return returned[route[4, 0:BLK]]


def solution(mesh):
    placed = (
        P(("geo", "slab"), None, None),
        P(("geo", "slab"), None, None),
        P(("geo", "slab"), None),
        P(("geo", "slab")),
        P(("geo", "slab"), None, None),
        P(("geo", "slab"), None),
        P(("geo", "slab")),
        P(None, "slab", None, None),
        P(),
        P(),
        P(),
        P(),
    )
    return jax.shard_map(
        local, mesh=mesh, in_specs=placed, out_specs=P(("geo", "slab"), None), check_vma=False
    )
```

```python
import functools
import math

import jax
import jax.numpy as jnp
import numpy as np
from jax import lax
from jax.experimental import pallas as pl
from jax.experimental.pallas import tpu as pltpu
from jax.sharding import PartitionSpec as P

C = 32
NX = 128
NY = 128
NZ = 128
MX = 64
MY = 64
MZ = 33
PB = 128
BLK = 128
SLABS = 64
PLANES = NX // SLABS
CAP = 6
SLOTS = SLABS * CAP
LINES = PLANES * NY
MROWS = 40
QROWS = 24
VMEM_LIMIT = 60 * 1024 * 1024

radius_scale = 0.7
spread_cells = 1.5
BF = jnp.bfloat16
F32 = jnp.float32


def split_np(table):
    table = np.asarray(table, np.float32)
    high = table.astype(jnp.bfloat16)
    low = (table - high.astype(np.float32)).astype(jnp.bfloat16)
    return high, low


def left_np(table):
    high, low = split_np(table)
    return np.concatenate([high, low, high], axis=1)


def right_np(table):
    high, low = split_np(table)
    return np.concatenate([high, high, low], axis=0)


def split(values):
    high = values.astype(BF)
    low = (values - high.astype(F32)).astype(BF)
    return high, low


def left_table(values):
    high = lax.reduce_precision(values, 8, 7)
    low = (values - high).astype(BF)
    high = high.astype(BF)
    return jnp.concatenate([high, low, high], axis=1)


def left3(values):
    high, low = split(values)
    return jnp.concatenate([high, low, high], axis=1)


def right3(values):
    high, low = split(values)
    return jnp.concatenate([high, high, low], axis=0)


def mm(left, right):
    return jnp.dot(left, right, preferred_element_type=F32)


def nt(left, right):
    return lax.dot_general(left, right, (((1,), (1,)), ((), ())), preferred_element_type=F32)


def kept(length, count):
    counter = np.arange(count)
    return np.where(counter < count // 2, counter, counter + length - count)


def tables():
    cells = np.arange(NY)
    ky = kept(NY, MY)
    angle = 2.0 * math.pi * ((ky[:, None] * cells[None, :]) % NY) / NY
    cos_y, sin_y = np.cos(angle), np.sin(angle)
    forward_y = np.concatenate([cos_y, -sin_y], axis=0)
    inverse_y = np.concatenate([cos_y.T, sin_y.T], axis=0) / NY
    z_angle = 2.0 * math.pi * ((np.arange(NZ)[:, None] * np.arange(MZ)[None, :]) % NZ) / NZ
    cos_z, sin_z = np.cos(z_angle), np.sin(z_angle)
    forward_z = np.zeros((2 * NZ, 128))
    forward_z[:NZ, :MZ] = cos_z
    forward_z[:NZ, 64 : 64 + MZ] = -sin_z
    forward_z[NZ:, :MZ] = sin_z
    forward_z[NZ:, 64 : 64 + MZ] = cos_z
    weight = np.where(np.arange(MZ) == 0, 1.0, 2.0) / NZ
    inverse_z = np.zeros((2, 2, 64, 2, NZ))
    for twin in range(2):
        inverse_z[0, twin, :MZ, twin, :] = (cos_z * weight[None, :]).T
        inverse_z[1, twin, :MZ, twin, :] = -(sin_z * weight[None, :]).T
    inverse_z = inverse_z.reshape(256, 256)
    kx = kept(NX, MX)
    owner = np.arange(SLABS)
    forward_x, inverse_x = [], []
    for part in (np.cos, np.sin):
        for plane in range(PLANES):
            turns = (kx[:, None] * (PLANES * owner + plane)[None, :]) % NX
            table = part(2.0 * math.pi * turns / NX)
            forward_x.append(table)
            inverse_x.append(table.T / NX)
    forward_x = np.concatenate(forward_x, axis=0)
    inverse_x = np.concatenate(inverse_x, axis=0)
    spread = np.zeros((2, PLANES, C, 2, C, C))
    for channel in range(C):
        for part in range(2):
            spread[part, :, channel, part, channel, :] = 1.0
    spread = spread.reshape(128, 2 * C * C)
    gather = np.zeros((2, 4, C, 2, PLANES, C))
    for channel in range(C):
        for part in range(2):
            gather[part, :, channel, part, :, channel] = 1.0
    gather = gather.reshape(256, 128)
    return (
        left_np(forward_y),
        left_np(inverse_y),
        right_np(forward_z),
        right_np(inverse_z),
        left_np(forward_x),
        left_np(inverse_x),
        np.asarray(np.concatenate([spread, spread], axis=0), jnp.bfloat16),
        np.asarray(np.concatenate([gather, gather], axis=0), jnp.bfloat16),
    )


def params(**extra):
    return pltpu.CompilerParams(vmem_limit_bytes=VMEM_LIMIT, **extra)


def cost(microseconds):
    return pl.CostEstimate(
        flops=0, transcendentals=0, bytes_accessed=int(microseconds * 2_000_000)
    )


def whole(shape):
    return pl.BlockSpec(shape, lambda *_: (0,) * len(shape))


SMEM = pl.BlockSpec(memory_space=pltpu.SMEM)


def routes_kernel(ed, el, dd, dl, out):
    rows = lax.broadcasted_iota(jnp.int32, (BLK, BLK), 0)
    cols = lax.broadcasted_iota(jnp.int32, (BLK, BLK), 1)

    def column(row):
        spread_row = jnp.broadcast_to(row.astype(F32), (BLK, BLK))
        return jnp.sum(jnp.where(rows == cols, spread_row, 0.0), axis=1, keepdims=True)

    def one(dest_r, line_r):
        dest_c = column(dest_r).astype(jnp.int32)
        line_c = column(line_r)
        same = dest_c == dest_r
        before_r = jnp.sum(jnp.where(same & (rows < cols), 1.0, 0.0), axis=0, keepdims=True)
        slot_r = dest_r * CAP + before_r.astype(jnp.int32)
        slot_c = column(slot_r).astype(jnp.int32)
        match = slot_c == lax.broadcasted_iota(jnp.int32, (BLK, SLOTS), 1)
        number = lax.broadcasted_iota(jnp.int32, (BLK, SLOTS), 0).astype(F32)
        filled = jnp.sum(jnp.where(match, 1.0, 0.0), axis=0, keepdims=True)
        source = jnp.sum(jnp.where(match, number, 0.0), axis=0, keepdims=True)
        line = jnp.sum(jnp.where(match, line_c, 0.0), axis=0, keepdims=True)
        return dest_r * 8 + before_r.astype(jnp.int32), filled, source.astype(jnp.int32), line.astype(jnp.int32)

    out[...] = jnp.zeros((8, SLOTS), jnp.int32)
    _, filled, source, line = one(ed[...], el[...])
    out[0:1, :] = jnp.where(filled > 0.5, source, BLK)
    out[1:2, :] = line
    slot, _, source, line = one(dd[...], dl[...])
    out[2:3, :] = source
    out[3:4, :] = line
    out[4:5, 0:BLK] = slot


def encode_kernel(route, feat, pos, out, terms):
    step = pl.program_id(0)

    @pl.when(step == 0)
    def _():
        terms[BLK] = jnp.zeros((C, NZ), F32)

    @pl.when(step < 8)
    def _():
        grid_cells = lax.broadcasted_iota(jnp.int32, (NZ, PB), 0).astype(F32)
        for b in range(16):
            a, o, t = pos[0, b : b + 1, :], pos[1, b : b + 1, :], pos[2, b : b + 1, :]
            radial = jnp.exp((a * a + o * o) * (-1.0 / (2.0 * radius_scale**2)))
            offset = grid_cells - (t + 1.0) * (0.5 * (NZ - 1))
            rows = jnp.exp(offset * offset * (-1.0 / (2.0 * spread_cells**2)))
            fh, fl = split(feat[b] * radial)
            kh, kl = split(rows)
            both = nt(jnp.concatenate([fh, fl], axis=0), kh)
            terms[step * 16 + b] = both[:C] + (both[C:] + nt(fh, kl))

    @pl.when(step >= 8)
    def _():
        base = (step - 8) * 48

        def put(i, carry):
            out[i] = terms[route[0, base + i]]
            return carry

        lax.fori_loop(0, 48, put, 0, unroll=8)


def queries_kernel(route, pos, out):
    lane = lax.broadcasted_iota(jnp.int32, (1, 128), 1)

    def peer(d, carry):
        tags = jnp.zeros((1, 128), F32)
        for r in range(CAP):
            s = d * CAP + r
            for part in range(3):
                out[d, 3 * r + part : 3 * r + part + 1, :] = pos[part, pl.ds(route[2, s], 1), :]
            tags = jnp.where(lane == r, route[3, s].astype(F32), tags)
            tags = jnp.where(lane == CAP + r, route[1, s].astype(F32), tags)
        out[d, 18:19, :] = tags
        out[d, 19:24, :] = jnp.zeros((5, 128), F32)
        return carry

    lax.fori_loop(0, SLABS, peer, 0, unroll=4)


def profile_kernel(pos, out):
    step = pl.program_id(0)
    grid_cells = lax.broadcasted_iota(jnp.int32, (NZ, PB), 0).astype(F32)

    def one(d, carry):
        for r in range(CAP):
            a = pos[d, 3 * r : 3 * r + 1, :]
            o = pos[d, 3 * r + 1 : 3 * r + 2, :]
            t = pos[d, 3 * r + 2 : 3 * r + 3, :]
            radial = jnp.exp((a * a + o * o) * (-1.0 / (2.0 * radius_scale**2)))
            offset = grid_cells - (t + 1.0) * (0.5 * (NZ - 1))
            rows = jnp.exp(offset * offset * (-1.0 / (2.0 * spread_cells**2))) * radial
            kh, kl = split(rows)
            out[d * CAP + r, :, 0:PB] = kh
            out[d * CAP + r, :, PB : 2 * PB] = kl
        return carry

    lax.fori_loop(0, 4, one, 0)


def forward_kernel(tags, got, dy, fz, latent, message, scratch):
    step = pl.program_id(0)

    @pl.when(step == 0)
    def _():
        latent[...] = jnp.zeros_like(latent)

    for q in range(8):
        for r in range(CAP):
            line = tags[step * 8 + q, CAP + r]
            start = pl.multiple_of(line * C, C)
            latent[pl.ds(start, C), :] += got[q * CAP + r]

    @pl.when(step == 7)
    def _():
        def quad(i, carry):
            plane = i // (C // 4)
            channel = (i % (C // 4)) * 4
            start = plane * NY * C + channel
            data = jnp.concatenate(
                [latent[pl.ds(start + n, NY, stride=C), :] for n in range(4)], axis=1
            )
            y = mm(dy[...], right3(data))
            x = jnp.concatenate(
                [
                    jnp.concatenate(
                        [y[:MY, n * NZ : n * NZ + NZ], y[MY:, n * NZ : n * NZ + NZ]], axis=1
                    )
                    for n in range(4)
                ],
                axis=0,
            )
            at = pl.multiple_of((plane * C + channel) * MY, MY)
            scratch[pl.ds(at, 4 * MY), :] = mm(left3(x), fz[...])
            return carry

        lax.fori_loop(0, PLANES * C // 4, quad, 0, unroll=4)

        def flip(j, carry):
            turned = jnp.transpose(scratch[pl.ds(j, PLANES * C, stride=MY), :])
            message[j, :, 0:64] = turned[:MROWS]
            message[j, :, 64:128] = turned[64 : 64 + MROWS]
            return carry

        lax.fori_loop(0, MY, flip, 0, unroll=8)


def planes_of(t, first_plane):
    u = jnp.where(first_plane, t[0:64], t[64:128])
    w = jnp.where(first_plane, t[128:192], t[192:256])
    return u, pltpu.roll(w, 64, 1)


def mix_rows(spec, weight, fx, spread, gather, ix, out, pitch, row, kz, count):
    lane = lax.broadcasted_iota(jnp.int32, (64, 128), 1)
    first_plane = (lane & 32) == 0
    real_part = lane < 64
    data = jnp.concatenate(
        [spec[pl.ds(row + n, SLABS, stride=pitch), :] for n in range(count)], axis=1
    )
    t = mm(fx[...], right3(data))
    rows = []
    for n in range(count):
        u, w = planes_of(t[:, n * 128 : n * 128 + 128], first_plane)
        rows.append(u + jnp.where(real_part, w, -w))
    sh, sl = split(jnp.concatenate(rows, axis=0))
    wide = mm(jnp.concatenate([sh, sl], axis=1), spread[...])
    rows = []
    for n in range(count):
        acc_re = jnp.zeros((64, 128), F32)
        acc_im = jnp.zeros((64, 128), F32)
        part = slice(n * 64, n * 64 + 64)
        for piece in range(8):
            re = slice(piece * 128, piece * 128 + 128)
            im = slice(C * C + piece * 128, C * C + piece * 128 + 128)
            w_re = weight[kz + n, :, re].astype(F32)
            w_im = weight[kz + n, :, im].astype(F32)
            acc_re += wide[part, re] * w_re - wide[part, im] * w_im
            acc_im += wide[part, re] * w_im + wide[part, im] * w_re
        rows.append(jnp.concatenate([acc_re, acc_im], axis=1))
    ah, al = split(jnp.concatenate(rows, axis=0))
    o = mm(jnp.concatenate([ah, al], axis=1), gather[...])
    data = jnp.concatenate([o[n * 64 : n * 64 + 64] for n in range(count)], axis=1)
    t = mm(ix[...], right3(data))
    for n in range(count):
        u, w = planes_of(t[:, n * 128 : n * 128 + 128], first_plane)
        out[pl.ds(row + n, SLABS, stride=pitch), :] = u + jnp.where(real_part, -w, w)


GROUPS = ((0, 16, 16), (16, 16, 16), (32, 1, 8))


def mix_kernel(
    message, weight_far, latent, fx, spread, gather, ix, kron, bias, out, base,
    spec_0, spec_1, spec_2, ready_0, ready_1, ready_2, weight, field,
    send_a, recv_a, send_b, recv_b, weight_sem, field_sem,
):
    specs, readies = (spec_0, spec_1, spec_2), (ready_0, ready_1, ready_2)
    me = lax.axis_index("slab")
    barrier = pltpu.get_barrier_semaphore()
    mesh_id = pl.DeviceIdType.MESH

    def greet(k, carry):
        peer = lax.rem(me + k, SLABS)
        pl.semaphore_signal(barrier, inc=1, device_id={"slab": peer}, device_id_type=mesh_id)
        return carry

    lax.fori_loop(1, SLABS, greet, 0)
    fetch = pltpu.make_async_copy(weight_far, weight, weight_sem)
    fetch.start()
    bring = pltpu.make_async_copy(latent, field, field_sem.at[0])
    bring.start()
    for group, (first, count, pitch) in enumerate(GROUPS):
        near = pl.multiple_of(me * pitch, 8)
        far = pl.multiple_of(me * MROWS + first, 8)
        specs[group][pl.ds(near, pitch), :] = message[pl.ds(far, pitch), :]
    pl.semaphore_wait(barrier, SLABS - 1)

    def scatter(source, target, send, recv, group, source_pitch, target_pitch, count):
        def go(k, carry):
            peer = lax.rem(me + lax.rem(k * 27, SLABS), SLABS)
            theirs = pl.multiple_of(peer * source_pitch[0] + source_pitch[1], 8)
            mine = pl.multiple_of(me * target_pitch[0] + target_pitch[1], 8)
            pltpu.make_async_remote_copy(
                src_ref=source.at[pl.ds(theirs, count)],
                dst_ref=target.at[pl.ds(mine, count)],
                send_sem=send.at[group],
                recv_sem=recv.at[group],
                device_id={"slab": peer},
                device_id_type=mesh_id,
            ).start()
            return carry

        lax.fori_loop(1, SLABS, go, 0)

    def settle(ref, sem, group, count):
        part = ref.at[pl.ds(0, (SLABS - 1) * count)]
        pltpu.make_async_copy(part, part, sem.at[group]).wait()

    for group, (first, count, pitch) in enumerate(GROUPS):
        scatter(message, specs[group], send_a, recv_a, group, (MROWS, first), (pitch, 0), count)
    bring.wait()

    def skip(n, carry):
        rows = pl.ds(pl.multiple_of(n * 256, 256), 256)
        field[rows, :] = mm(kron[...], right3(field[rows, :])) + bias[...]
        return carry

    lax.fori_loop(0, LINES * C // 256, skip, 0)
    leave = pltpu.make_async_copy(field, base, field_sem.at[1])
    leave.start()
    fetch.wait()
    for group, (first, count, pitch) in enumerate(GROUPS):
        spec, ready = specs[group], readies[group]
        settle(spec, recv_a, group, count)
        if count == 1:
            ready[...] = jnp.zeros_like(ready)
            mix_rows(spec, weight, fx, spread, gather, ix, ready, pitch, 0, first, 1)
        else:

            def four(i, carry):
                row = 4 * i
                mix_rows(spec, weight, fx, spread, gather, ix, ready, pitch, row, first + row, 4)
                return carry

            lax.fori_loop(0, count // 4, four, 0)
        scatter(ready, out, send_b, recv_b, group, (pitch, 0), (MROWS, first), count)
        near = pl.multiple_of(me * pitch, 8)
        far = pl.multiple_of(me * MROWS + first, 8)
        out[pl.ds(far, pitch), :] = ready[pl.ds(near, pitch), :]
    for group, (first, count, pitch) in enumerate(GROUPS):
        settle(message, send_a, group, count)
        settle(readies[group], send_b, group, count)
        settle(out, recv_b, group, count)
    leave.wait()


def decode_kernel(tags, inverse, base, profile, iy, iz, dw, ow, out, modes, hidden):
    step = pl.program_id(0)

    @pl.when(step == 0)
    def _():
        lane = lax.broadcasted_iota(jnp.int32, (NY, 128), 1)
        real_part = lane < 64

        def clear(n, carry):
            modes[pl.ds(pl.multiple_of(n * 64 + 32, 32), 32), :] = jnp.zeros((32, 128), F32)
            return carry

        lax.fori_loop(0, NY, clear, 0, unroll=8)

        def planes(i, carry):
            data = jnp.concatenate(
                [inverse[pl.ds(i * 3 + n, MY, stride=MROWS), :] for n in range(3)], axis=1
            )
            t = mm(iy[...], right3(data))
            for n in range(3):
                cols = slice(n * 128, n * 128 + 128)
                w = pltpu.roll(t[NY:, cols], 64, 1)
                modes[pl.ds(i * 3 + n, NY, stride=64), :] = t[:NY, cols] + jnp.where(
                    real_part, -w, w
                )
            return carry

        lax.fori_loop(0, MZ // 3, planes, 0, unroll=True)

        def columns(i, carry):
            rows = []
            for n in range(4):
                at = pl.multiple_of((i * 4 + n) * 128, 128)
                turned = jnp.transpose(modes[pl.ds(at, 128), :])
                rows.append(jnp.concatenate([turned[:64], turned[64:]], axis=1))
            s = mm(left3(jnp.concatenate(rows, axis=0)), iz[...])
            for n in range(4):
                for plane in range(PLANES):
                    for twin in range(2):
                        at = pl.multiple_of((plane * NY + 2 * (i * 4 + n) + twin) * C, C)
                        top = n * 64 + plane * C
                        value = s[top : top + C, twin * NZ : twin * NZ + NZ] + base[pl.ds(at, C), :]
                        hidden[pl.ds(at, C), :] = jax.nn.gelu(value)
            return carry

        lax.fori_loop(0, NY // 8, columns, 0, unroll=2)

    for pair in range(2):
        sides = []
        for half in range(2):
            near = []
            for i in range(6):
                q = (pair * 2 + half) * 6 + i
                line = tags[step * 4 + pair * 2 + half, i]
                hh, hl = split(hidden[pl.ds(pl.multiple_of(line * C, C), C), :])
                both = mm(jnp.concatenate([hh, hl], axis=0), profile[q])
                near.append(both[:C, :PB] + (both[C:, :PB] + both[:C, PB:]))
            sides.append(jnp.concatenate(near, axis=0))
        act = jax.nn.gelu(mm(dw[...], right3(jnp.concatenate(sides, axis=1))))
        result = mm(ow[...], right3(act))
        for half in range(2):
            d = pair * 2 + half
            out[d * 8 : d * 8 + CAP, :] = result[:, half * PB : half * PB + PB]


def reply_kernel(answers, out, send_sem, recv_sem):
    me = lax.axis_index("slab")
    barrier = pltpu.get_barrier_semaphore()
    mesh_id = pl.DeviceIdType.MESH

    def greet(k, carry):
        peer = lax.rem(me + k, SLABS)
        pl.semaphore_signal(barrier, inc=1, device_id={"slab": peer}, device_id_type=mesh_id)
        return carry

    lax.fori_loop(1, SLABS, greet, 0)
    here = pl.multiple_of(me * 8, 8)
    out[pl.ds(here, 8), :] = answers[pl.ds(here, 8), :]
    pl.semaphore_wait(barrier, SLABS - 1)

    def go(k, carry):
        peer = lax.rem(me + lax.rem(k * 27, SLABS), SLABS)
        there = pl.multiple_of(peer * 8, 8)
        pltpu.make_async_remote_copy(
            src_ref=answers.at[pl.ds(there, CAP)],
            dst_ref=out.at[pl.ds(here, CAP)],
            send_sem=send_sem,
            recv_sem=recv_sem,
            device_id={"slab": peer},
            device_id_type=mesh_id,
        ).start()
        return carry

    lax.fori_loop(1, SLABS, go, 0)
    everything = pl.ds(0, (SLABS - 1) * CAP)
    came, sent = out.at[everything], answers.at[everything]
    pltpu.make_async_copy(came, came, recv_sem).wait()
    pltpu.make_async_copy(sent, sent, send_sem).wait()


def local(
    enc_feat,
    enc_pos,
    enc_dest,
    enc_line,
    dec_pos,
    dec_dest,
    dec_line,
    mode_weight,
    skip_weight,
    skip_bias,
    dec_weight,
    out_weight,
):
    forward_y, inverse_y, forward_z, inverse_z, forward_x, inverse_x, spread, gather = tables()
    exchange = functools.partial(
        lax.all_to_all, axis_name="slab", split_axis=0, concat_axis=0, tiled=True
    )
    route = pl.pallas_call(
        routes_kernel, out_shape=jax.ShapeDtypeStruct((8, SLOTS), jnp.int32), name="routes"
    )(
        enc_dest.reshape(1, BLK),
        enc_line.reshape(1, BLK),
        dec_dest.reshape(1, BLK),
        dec_line.reshape(1, BLK),
    )
    queries = pl.pallas_call(
        queries_kernel,
        out_shape=jax.ShapeDtypeStruct((SLABS, QROWS, 128), F32),
        in_specs=[SMEM, whole((3, BLK, PB))],
        out_specs=whole((SLABS, QROWS, 128)),
        name="queries",
    )(route, jnp.transpose(dec_pos, (1, 0, 2)))
    packed = pl.pallas_call(
        encode_kernel,
        out_shape=jax.ShapeDtypeStruct((SLOTS, C, NZ), F32),
        grid=(16,),
        in_specs=[
            SMEM,
            pl.BlockSpec((16, C, PB), lambda i: (jnp.minimum(i, 7), 0, 0)),
            pl.BlockSpec((3, 16, PB), lambda i: (0, jnp.minimum(i, 7), 0)),
        ],
        out_specs=pl.BlockSpec((48, C, NZ), lambda i: (jnp.maximum(i - 8, 0), 0, 0)),
        scratch_shapes=[pltpu.VMEM((BLK + 1, C, NZ), F32)],
        compiler_params=params(),
        cost_estimate=cost(12),
        name="encode",
    )(route, enc_feat, jnp.transpose(enc_pos, (1, 0, 2)))
    got_queries = exchange(queries)
    got_terms = exchange(packed)
    tags = got_queries[:, 18, 0 : 2 * CAP].astype(jnp.int32)
    profile = pl.pallas_call(
        profile_kernel,
        out_shape=jax.ShapeDtypeStruct((SLOTS, NZ, 2 * PB), BF),
        grid=(16,),
        in_specs=[pl.BlockSpec((4, QROWS, PB), lambda i: (i, 0, 0))],
        out_specs=pl.BlockSpec((24, NZ, 2 * PB), lambda i: (i, 0, 0)),
        compiler_params=params(),
        cost_estimate=cost(25),
        name="profile",
    )(got_queries)
    tags, profile = lax.optimization_barrier((tags, profile))
    skip_wide = left_table(jnp.kron(jnp.eye(8, dtype=F32), skip_weight.T))
    skip_bias_wide = jnp.tile(skip_bias, 8)[:, None]
    dec_wide = left_table(jnp.kron(jnp.eye(CAP, dtype=F32), dec_weight.T))
    out_wide = left_table(jnp.kron(jnp.eye(CAP, dtype=F32), out_weight[None, :]))
    latent, message = pl.pallas_call(
        forward_kernel,
        out_shape=(
            jax.ShapeDtypeStruct((LINES * C, NZ), F32),
            jax.ShapeDtypeStruct((MY, MROWS, 128), F32),
        ),
        grid=(8,),
        in_specs=[
            SMEM,
            pl.BlockSpec((48, C, NZ), lambda i: (i, 0, 0)),
            whole((2 * MY, 3 * NY)),
            whole((6 * NZ, 128)),
        ],
        out_specs=(whole((LINES * C, NZ)), whole((MY, MROWS, 128))),
        scratch_shapes=[pltpu.VMEM((PLANES * C * MY, 128), F32)],
        compiler_params=params(),
        name="forward",
    )(tags, got_terms, forward_y, forward_z)
    weight = jnp.transpose(mode_weight.reshape(MX, MZ, 2 * C * C), (1, 0, 2))
    vm = pl.BlockSpec(memory_space=pltpu.VMEM)
    far = pl.BlockSpec(memory_space=pl.ANY)
    inverse, base = pl.pallas_call(
        mix_kernel,
        out_shape=(
            jax.ShapeDtypeStruct((SLABS * MROWS, 128), F32),
            jax.ShapeDtypeStruct((LINES * C, NZ), F32),
        ),
        in_specs=[vm, far, far, vm, vm, vm, vm, vm, vm],
        out_specs=(vm, far),
        scratch_shapes=[
            *[pltpu.VMEM((SLABS * pitch, 128), F32) for _, _, pitch in GROUPS],
            *[pltpu.VMEM((SLABS * pitch, 128), F32) for _, _, pitch in GROUPS],
            pltpu.VMEM((MZ, MX, 2 * C * C), BF),
            pltpu.VMEM((LINES * C, NZ), F32),
            pltpu.SemaphoreType.DMA((3,)),
            pltpu.SemaphoreType.DMA((3,)),
            pltpu.SemaphoreType.DMA((3,)),
            pltpu.SemaphoreType.DMA((3,)),
            pltpu.SemaphoreType.DMA,
            pltpu.SemaphoreType.DMA((2,)),
        ],
        compiler_params=params(collective_id=0, has_side_effects=True),
        name="mix",
    )(
        message.reshape(SLABS * MROWS, 128),
        weight,
        latent,
        forward_x,
        spread,
        gather,
        inverse_x,
        skip_wide,
        skip_bias_wide,
    )
    answers = pl.pallas_call(
        decode_kernel,
        out_shape=jax.ShapeDtypeStruct((SLABS * 8, PB), F32),
        grid=(16,),
        in_specs=[
            SMEM,
            whole((MY * MROWS, 128)),
            whole((LINES * C, NZ)),
            pl.BlockSpec((24, NZ, 2 * PB), lambda i: (i, 0, 0)),
            whole((2 * NY, 192)),
            whole((768, 2 * NZ)),
            whole((CAP * C, 3 * CAP * C)),
            whole((CAP, 3 * CAP * C)),
        ],
        out_specs=pl.BlockSpec((32, PB), lambda i: (i, 0)),
        scratch_shapes=[
            pltpu.VMEM((NY * 64, 128), F32),
            pltpu.VMEM((LINES * C, NZ), F32),
        ],
        compiler_params=params(),
        name="decode",
    )(
        tags,
        inverse,
        base,
        profile,
        inverse_y,
        inverse_z,
        dec_wide,
        out_wide,
    )
    returned = pl.pallas_call(
        reply_kernel,
        out_shape=jax.ShapeDtypeStruct((SLABS * 8, PB), F32),
        in_specs=[vm],
        out_specs=vm,
        scratch_shapes=[pltpu.SemaphoreType.DMA, pltpu.SemaphoreType.DMA],
        compiler_params=params(collective_id=1, has_side_effects=True),
        name="reply",
    )(answers)
    return returned[route[4, 0:BLK]]


def solution(mesh):
    placed = (
        P(("geo", "slab"), None, None),
        P(("geo", "slab"), None, None),
        P(("geo", "slab"), None),
        P(("geo", "slab")),
        P(("geo", "slab"), None, None),
        P(("geo", "slab"), None),
        P(("geo", "slab")),
        P(None, "slab", None, None),
        P(),
        P(),
        P(),
        P(),
    )
    return jax.shard_map(
        local, mesh=mesh, in_specs=placed, out_specs=P(("geo", "slab"), None), check_vma=False
    )
```
